32 devices in a mesh: gx: 2 (over core), gy: 4 (over y, x), gz: 4 (over z).
Axes of the slice: x: 2, y: 2, z: 4, core: 2. Of those that a mesh axis runs over, the one named last changes fastest.
Arguments:
- adj_prev: float32 [16, 32, 2048], P('gx', 'gz', 'gy'), may hold values from -6 to 6
- adj_cur: float32 [16, 32, 2048], P('gx', 'gz', 'gy'), may hold values from -6 to 6
- velocity: float32 [16, 32, 2048], P('gx', 'gz', 'gy'), may hold values from 1.5 to 4.4
- fwd_accel: float32 [2, 16, 32, 2048], P(None, 'gx', 'gz', 'gy'), may hold values from -6 to 6
- residuals: float32 [2, 8192], P(None, ('gx', 'gy', 'gz')), may hold values from -6 to 6
- recv_tile: int32 [8192, 1], P(('gx', 'gy', 'gz')), may hold values from 0 to 7; in each aligned block of 256 rows (0 to 255, 256 to 511, ...) at most 64 rows name the same one
- recv_cell: int32 [8192], P(('gx', 'gy', 'gz')), may hold values from 0 to 32767
Outputs:
- adj_prev_out: float32 [16, 32, 2048], P('gx', 'gz', 'gy')
- adj_cur_out: float32 [16, 32, 2048], P('gx', 'gz', 'gy')
- gradient: float32 [16, 32, 2048], P('gx', 'gz', 'gy')
The draws below stay inside these ranges and needn't reach their ends.
Inputs may be any that keep to these rules, and one draw needn't show every extreme that they name: `recv_tile`: of the 256 receivers held by one device, at most 64 lie in one tile, and in every draw some tile takes exactly 64 of some device's receivers. `recv_cell`: cells are numbered first lateral slowest, then depth, then second lateral.
All inputs are finite; a program needn't handle non-finite values.
Results may differ from the reference program's by a relative error of at most 0.000026.
Values sent between devices are 32-bit elements; how exact they have to be, the bound alone decides.
No kernel may reach another device: no remote copies, remote signals or barrier semaphores. Data moves between devices by JAX's collectives and lax.ppermute only.
A program may use at most 64 MiB of HBM per device.

```python
import math
import jax
import jax.numpy as jnp
import numpy as np

CX = 8
CZ = 8
CY = 512
R_DEV = 256
TILES = 8
CAP = 64
RECV = 8192
NX = 16
NZ = 32
NY = 2048
N_GY = 4
N_GZ = 4


def touch_ends(values, key, smallest, top_value):
    place = [jax.random.randint(jax.random.fold_in(key, axis), (), 0, length) for axis, length in enumerate(values.shape)]
    widest = values.shape.index(max(values.shape))
    neighbour = place[:widest] + [(place[widest] + 1) % values.shape[widest]] + place[widest + 1:]
    return values.at[tuple(place)].set(smallest).at[tuple(neighbour)].set(top_value)


def shard_levels(key, dims, pieces, least, largest):
    factor_of = 1.0
    for position, parts in pieces:
        heights = jax.random.uniform(jax.random.fold_in(jax.random.fold_in(key, 6), position), (parts,), jnp.float32, least / len(pieces), largest / len(pieces))
        factor_of = factor_of * jnp.repeat(jnp.exp(heights), dims[position] // parts).reshape((-1,) + (1,) * (len(dims) - 1 - position))
    return factor_of


def shared_out(stream_key, own, number, rows, number_of, top, reach, lean):
    sequence = jax.random.permutation(stream_key, number_of)
    heavy_load, usual = load_shares(number_of, rows * top, reach, lean, True), load_shares(number_of, rows * top, reach, lean, False)
    places = jnp.arange(number_of)

    def named(sizes, rotation):
        used = int((sizes > 0).sum())
        fixed = max(1, used // 4)
        passed = fixed + (places - fixed + rotation * (used - fixed)) % max(1, number_of - fixed)
        return jnp.zeros((number_of,), jnp.int32).at[sequence[jnp.where(places < fixed, places, passed)]].set(jnp.asarray(sizes, jnp.int32))

    sizes = jnp.where(number % 4 == 0, named(heavy_load, number // 4), named(usual, number - number // 4 - 1))
    mixed = jax.random.permutation(jax.random.fold_in(own, 3), number_of)
    giver, taker = mixed[0:number_of // 2 * 2:2], mixed[1:number_of // 2 * 2:2]
    slack = jnp.minimum(sizes[giver] - 1, reach - sizes[taker]) // 2
    slack = jnp.where((giver == sequence[0]) | (taker == sequence[0]) | (sizes[taker] == 0), 0, jnp.maximum(slack, 0))
    passed = jax.random.randint(jax.random.fold_in(own, 4), (number_of // 2,), 0, 1 << 20) % (slack + 1)
    sizes = sizes.at[giver].add(-passed).at[taker].add(passed)
    items = jnp.searchsorted(jnp.cumsum(sizes), jnp.arange(rows * top), side="right").astype(jnp.int32)
    listing = items.reshape(top, rows).T
    listing = listing[jax.random.permutation(jax.random.fold_in(own, 1), rows)]
    rotation = jax.random.randint(jax.random.fold_in(own, 2), (rows, 1), 0, top)
    return jnp.take_along_axis(listing, (jnp.arange(top)[None, :] + rotation) % top, axis=1)


def load_shares(count, total, limit, slope, full):
    weights = [(1 << 20) // math.isqrt(grade ** slope) + 1 for grade in range(1, count + 1)]
    largest = limit if full else min(limit, max(-(-total // count), total * weights[0] // sum(weights)))
    least = 1 if total - largest >= count - 1 else 0
    holding, rest = [largest] + [least] * (count - 1), total - largest - least * (count - 1)
    while rest > 0:
        movable = [i for i in range(1, count) if holding[i] < largest] or [i for i in range(1, count) if holding[i] < limit]
        pool, left = sum([weights[i] for i in movable]), rest
        for i in movable:
            more = min(limit - holding[i], max(1, left * weights[i] // pool), rest)
            holding[i] = holding[i] + more
            rest = rest - more
    return np.array(holding)


def normal_values(rng, extent, spread, most, split=(), held_as=jnp.bfloat16):
    values = jax.random.normal(rng, extent, jnp.float32) * spread
    if len(split) > 0:
        values = shard_levels(rng, extent, split, -0.22, 0.18) * values
    return jnp.clip(values, min=-most, max=most).astype(held_as)


def setup_inputs(seed: int = 0) -> dict:
    key_list = jax.random.split(jax.random.key(seed), 8)
    adj_prev = normal_values(key_list[0], (NX, NZ, NY), 1.0, 6.0, ((0, 2), (1, 4), (2, 4)), jnp.float32)
    adj_cur = normal_values(key_list[1], (NX, NZ, NY), 1.0, 6.0, ((0, 2), (1, 4), (2, 4)), jnp.float32)
    velocity = jnp.clip(jnp.exp(math.log(4.4) - 1.0761395 * jax.random.uniform(key_list[2], (NX, NZ, NY), jnp.float32) ** shard_levels(key_list[2], (NX, NZ, NY), ((0, 2), (1, 4), (2, 4)), -0.2, 0.2)), 1.5, 4.4)
    fwd_accel = normal_values(key_list[3], (2, NX, NZ, NY), 1.0, 6.0, ((1, 2), (2, 4), (3, 4)), jnp.float32)
    residuals = normal_values(key_list[4], (2, RECV), 1.0, 6.0, ((1, 32),), jnp.float32)
    recv_tile_keys = jax.random.split(jax.random.fold_in(key_list[5], 1), RECV // R_DEV)
    recv_tile_turns = jax.random.permutation(jax.random.fold_in(key_list[5], 3), RECV // R_DEV)
    recv_tile = jax.vmap(lambda own, number: shared_out(jax.random.fold_in(key_list[5], 2), own, number, R_DEV, TILES, 1, CAP, 2))(recv_tile_keys, recv_tile_turns).reshape((RECV, 1))
    recv_cell = touch_ends(jax.random.randint(key_list[6], (RECV,), 0, CX * CZ * CY), jax.random.fold_in(key_list[6], 1), 0, (CX * CZ * CY) - 1).astype(jnp.int32)
    return {"adj_prev": adj_prev, "adj_cur": adj_cur, "velocity": velocity, "fwd_accel": fwd_accel, "residuals": residuals, "recv_tile": recv_tile, "recv_cell": recv_cell}


stencil_weights = (-205.0 / 72.0, 8.0 / 5.0, -1.0 / 5.0, 8.0 / 315.0, -1.0 / 560.0)
courant_scale = 0.1


def laplace_axes(along_x, along_z, along_y):
    size_x = along_z.shape[0]
    size_z = along_x.shape[1]
    size_y = along_x.shape[2]
    centre = along_x[4:4 + size_x]
    total = (3.0 * stencil_weights[0]) * centre
    for offset in range(1, 5):
        factor = stencil_weights[offset]
        total = total + factor * (along_x[4 + offset:4 + offset + size_x] + along_x[4 - offset:4 - offset + size_x]
                                  + along_z[:, 4 + offset:4 + offset + size_z] + along_z[:, 4 - offset:4 - offset + size_z]
                                  + along_y[:, :, 4 + offset:4 + offset + size_y] + along_y[:, :, 4 - offset:4 - offset + size_y])
    return total


def reference(adj_prev, adj_cur, velocity, fwd_accel, residuals, recv_tile, recv_cell):
    sender = jnp.arange(residuals.shape[1], dtype=jnp.int32) // R_DEV
    layer = sender % N_GZ
    target = recv_tile[:, 0].astype(jnp.int32)
    tile_x = target // N_GY
    tile_y = target % N_GY
    local_x = recv_cell // (CZ * CY)
    local_z = (recv_cell // CY) % CZ
    local_y = recv_cell % CY
    target_cell = ((tile_x * CX + local_x) * NZ + layer * CZ + local_z) * NY + tile_y * CY + local_y
    speed_sq = (velocity * courant_scale) ** 2
    weight = -2.0 / (velocity * velocity * velocity)
    gradient = jnp.zeros_like(velocity)
    previous = adj_prev
    current = adj_cur
    for moment in range(2):
        padded = jnp.pad(current, 4)
        laplacian = laplace_axes(padded[:, 4:-4, 4:-4], padded[4:-4, :, 4:-4], padded[4:-4, 4:-4, :])
        source = jnp.zeros((NX * NZ * NY,), jnp.float32).at[target_cell].add(residuals[moment]).reshape(velocity.shape)
        advanced = 2.0 * current - previous + speed_sq * laplacian + source
        gradient = gradient + weight * fwd_accel[moment] * advanced
        previous = current
        current = advanced
    return previous, current, gradient
```

```python
import functools
import jax
import jax.numpy as jnp
from jax import lax
from jax.experimental import pallas as pl
from jax.experimental.pallas import tpu as pltpu
from jax.sharding import PartitionSpec as P

stencil_weights = (-205.0 / 72.0, 8.0 / 5.0, -1.0 / 5.0, 8.0 / 315.0, -1.0 / 560.0)
courant_scale = 0.1
LANES = 128
F32 = jnp.float32
BF16 = jnp.bfloat16
VMEM = pl.BlockSpec(memory_space=pltpu.VMEM)


def pair_swaps(size, offset):
    pairs = []
    for i in range(offset, size - 1, 2):
        pairs += [(i, i + 1), (i + 1, i)]
    return pairs


def xor_swaps(size, bits):
    return [(i, i ^ bits) for i in range(size)]


def pack_kernel(cur_ref, res_ref, tile_ref, cell_ref, even_ref, odd_ref, own_ref, sem):
    blocks = cur_ref.shape[2] // LANES
    is_odd = lax.rem(lax.axis_index("gy"), 2)
    last = (blocks - 1) * LANES
    start_even = pl.multiple_of((1 - is_odd) * last, LANES)
    start_odd = pl.multiple_of(is_odd * last, LANES)
    size_x = cur_ref.shape[0]
    copies = (
        pltpu.make_async_copy(cur_ref.at[:, :, pl.ds(start_even, LANES)], even_ref.at[0:size_x], sem.at[0]),
        pltpu.make_async_copy(cur_ref.at[:, :, pl.ds(start_odd, LANES)], odd_ref.at[0:size_x], sem.at[1]),
    )
    for copy in copies:
        copy.start()
    tile = tile_ref[...].astype(F32)
    cell = cell_ref[...].astype(F32)
    rows = (
        res_ref[0:1, 0:LANES], res_ref[0:1, LANES:],
        res_ref[1:2, 0:LANES], res_ref[1:2, LANES:],
        tile[0:1], tile[1:2], cell[0:1], cell[1:2],
    )
    payload = jnp.concatenate(rows, axis=0)
    even_ref[size_x] = payload
    odd_ref[size_x] = payload
    own_ref[0] = payload
    for copy in copies:
        copy.wait()


def pack(cur, residuals, tile, cell):
    size_x, size_z, _ = cur.shape
    message = jax.ShapeDtypeStruct((size_x + 1, size_z, LANES), F32)
    return pl.pallas_call(
        pack_kernel,
        out_shape=(message, message, jax.ShapeDtypeStruct((1, 8, LANES), F32)),
        in_specs=[pl.BlockSpec(memory_space=pl.ANY), VMEM, VMEM, VMEM],
        out_specs=(VMEM, VMEM, VMEM),
        scratch_shapes=[pltpu.SemaphoreType.DMA((2,))],
        name="pack",
    )(cur, residuals, tile, cell)


def scatter_kernel(picks, shape, *refs):
    blocks, (out_ref, left_ref, right_ref) = refs[: len(picks)], refs[len(picks) :]
    size_x, size_z, size_y = shape
    rows = size_x * size_z
    mine = (lax.axis_index("gx") * lax.axis_size("gy") + lax.axis_index("gy")).astype(F32)
    row_iota = lax.broadcasted_iota(jnp.int32, (rows, LANES), 0)
    column_iota = lax.broadcasted_iota(jnp.int32, (size_y, LANES), 0)
    place = 0
    for ref, pick in zip(blocks, picks):
        block = ref[pick]
        cell = block[6:8].astype(jnp.int32)
        column = lax.rem(cell, size_y)
        row = jnp.where(block[4:6] == mine, lax.div(cell, size_y), -1)
        high = block[0:4].astype(BF16).astype(F32)
        rest = block[0:4] - high
        middle = rest.astype(BF16).astype(F32)
        low = rest - middle
        for half in range(2):
            lanes = slice(place, place + LANES)
            hit = row_iota == row[half : half + 1]
            for moment in range(2):
                line = 2 * moment + half
                for piece, value in enumerate((high, middle, low)):
                    top = (3 * moment + piece) * rows
                    left_ref[top : top + rows, lanes] = jnp.where(hit, value[line : line + 1], 0.0).astype(BF16)
            right_ref[:, lanes] = jnp.where(column_iota == column[half : half + 1], 1.0, 0.0).astype(BF16)
            place += LANES
    total = lax.dot_general(
        left_ref[...], right_ref[...], (((1,), (1,)), ((), ())), preferred_element_type=F32
    )
    for moment in range(2):
        base = 3 * moment * rows
        field = total[base : base + rows] + (total[base + rows : base + 2 * rows] + total[base + 2 * rows : base + 3 * rows])
        out_ref[moment] = field.reshape(shape)


def scatter(blocks, picks, shape):
    count = 2 * LANES * len(picks)
    rows = shape[0] * shape[1]
    return pl.pallas_call(
        functools.partial(scatter_kernel, picks, shape),
        out_shape=jax.ShapeDtypeStruct((2,) + shape, F32),
        in_specs=[VMEM] * len(blocks),
        out_specs=VMEM,
        scratch_shapes=[pltpu.VMEM((6 * rows, count), BF16), pltpu.VMEM((shape[2], count), BF16)],
        name="scatter",
    )(*blocks)


def laplacian_blocks(sizes, cur_ref, x_refs, z_refs, y_refs):
    size_x, size_z, size_y = cur_ref.shape
    places = [lax.axis_index(name) for name in ("gx", "gz", "gy")]
    count_x, count_z, count_y = sizes
    odd = [lax.rem(place, 2) == 1 for place in places]
    shape = (size_x, size_z, LANES)
    layer = lax.broadcasted_iota(jnp.int32, shape, 1)
    lane = lax.broadcasted_iota(jnp.int32, shape, 2)

    def side(parts, is_odd, before):
        first, second = (parts[0], parts[1]) if before else (parts[1], parts[0])
        return jnp.where(is_odd, first, second)

    ends = []
    for before in (True, False):
        parts = [ref[0:size_x] for ref in y_refs]
        at_edge = places[2] == (0 if before else count_y - 1)
        ends.append(jnp.where(at_edge, 0.0, side(parts, odd[2], before)))
    columns = [cur_ref[:, :, j : j + LANES] for j in range(0, size_y, LANES)]
    columns = [ends[0]] + columns + [ends[1]]
    lower = layer < 4
    from_even = jnp.logical_xor(lower, odd[1])
    for j in range(size_y // LANES):
        where = slice(j * LANES, (j + 1) * LANES)
        centre, left, right = columns[j + 1], columns[j], columns[j + 2]
        halves = []
        for before in (True, False):
            layers = slice(size_x - 4, size_x) if before else slice(0, 4)
            parts = [ref[layers, :, where] for ref in x_refs]
            if len(parts) == 1:
                parts.append(jnp.zeros_like(parts[0]))
            halves.append(side(parts, odd[0], before))
        along_x = jnp.concatenate([halves[0], centre, halves[1]], axis=0)
        beyond = jnp.where(from_even, z_refs[0][:, :, where], z_refs[1][:, :, where])
        total = (3.0 * stencil_weights[0]) * centre
        for offset in range(1, 5):
            near = along_x[4 + offset : 4 + offset + size_x] + along_x[4 - offset : 4 - offset + size_x]
            near += pltpu.roll(jnp.where(layer >= offset, centre, beyond), size_z - offset, 1)
            near += pltpu.roll(jnp.where(layer < size_z - offset, centre, beyond), offset, 1)
            near += pltpu.roll(jnp.where(lane >= offset, centre, right), LANES - offset, 2)
            near += pltpu.roll(jnp.where(lane < LANES - offset, centre, left), offset, 2)
            total += stencil_weights[offset] * near
        yield where, centre, total


def first_kernel(sizes, count_x, cur_ref, prev_ref, vel_ref, src_ref, *refs):
    x_refs, refs = refs[:count_x], refs[count_x:]
    z_refs, y_refs, (next_ref, even_ref, odd_ref) = refs[:2], refs[2:4], refs[4:]
    for where, centre, laplacian in laplacian_blocks(sizes, cur_ref, x_refs, z_refs, y_refs):
        scaled = vel_ref[:, :, where] * courant_scale
        next_ref[:, :, where] = (
            2.0 * centre - prev_ref[:, :, where] + scaled * scaled * laplacian + src_ref[0, :, :, where]
        )
    is_odd = lax.rem(lax.axis_index("gy"), 2) == 1
    first, last = next_ref[:, :, 0:LANES], next_ref[:, :, next_ref.shape[2] - LANES :]
    even_ref[...] = jnp.where(is_odd, first, last)
    odd_ref[...] = jnp.where(is_odd, last, first)


def second_kernel(sizes, count_x, cur_ref, prev_ref, vel_ref, src_ref, accel_ref, *refs):
    x_refs, refs = refs[:count_x], refs[count_x:]
    z_refs, y_refs, (next_ref, gradient_ref) = refs[:2], refs[2:4], refs[4:]
    for where, centre, laplacian in laplacian_blocks(sizes, cur_ref, x_refs, z_refs, y_refs):
        velocity = vel_ref[:, :, where]
        scaled = velocity * courant_scale
        advanced = 2.0 * centre - prev_ref[:, :, where] + scaled * scaled * laplacian + src_ref[1, :, :, where]
        next_ref[:, :, where] = advanced
        weight = -2.0 / (velocity * velocity * velocity)
        gradient_ref[:, :, where] = weight * accel_ref[0, :, :, where] * centre + weight * accel_ref[1, :, :, where] * advanced


def bucketed(residuals, target, cell, tile_count):
    held_count = residuals.shape[1]
    capacity = max(2, 2 * held_count // tile_count)
    one_hot = (target[:, None] == jnp.arange(tile_count, dtype=jnp.int32)[None, :]).astype(jnp.int32)
    earlier = jnp.cumsum(one_hot, axis=0) - one_hot
    slot_index = target * capacity + jnp.sum(one_hot * earlier, axis=1)
    payload = jnp.stack([residuals[0], residuals[1], cell.astype(F32)])
    outgoing = jnp.zeros((3, tile_count * capacity), F32).at[:, slot_index].set(payload)
    incoming = lax.all_to_all(outgoing, ("gx", "gy"), split_axis=1, concat_axis=1, tiled=True)
    block = 2 * LANES
    count = -(-incoming.shape[1] // block)
    incoming = jnp.pad(incoming, ((0, 0), (0, count * block - incoming.shape[1])))
    mine = (lax.axis_index("gx") * lax.axis_size("gy") + lax.axis_index("gy")).astype(F32)
    parts = jnp.concatenate([incoming[:2], jnp.full((1, count * block), mine), incoming[2:]])
    return parts.reshape(4, count, 2, LANES).transpose(1, 0, 2, 3).reshape(count, 8, LANES)


def shards(adj_prev, adj_cur, velocity, fwd_accel, residuals, recv_tile, recv_cell):
    count_x, count_z, count_y = sizes = tuple(lax.axis_size(name) for name in ("gx", "gz", "gy"))
    shape = velocity.shape
    target = recv_tile[:, 0]

    def halos(value):
        along_x = [lax.ppermute(value, "gx", pair_swaps(count_x, 0))]
        if count_x > 2:
            along_x.append(lax.ppermute(value, "gx", pair_swaps(count_x, 1)))
        along_z = [lax.ppermute(value, "gz", pair_swaps(count_z, offset)) for offset in range(2)]
        return along_x + along_z

    even_face, odd_face, own = pack(
        adj_cur, residuals, target.reshape(2, LANES), recv_cell.reshape(2, LANES)
    )
    if count_x == 2 and count_y == 4:
        even = lax.ppermute(even_face, "gy", xor_swaps(4, 1))
        odd = lax.ppermute(odd_face, "gy", xor_swaps(4, 3))
        far = lax.ppermute(own, "gy", xor_swaps(4, 2))
        current, even_face, odd_face, own = lax.optimization_barrier((adj_cur, even_face, odd_face, own))
        around = halos(current)
        swap = functools.partial(lax.ppermute, axis_name="gx", perm=pair_swaps(2, 0))
        same = [own, far, even, odd]
        blocks = same + [swap(block) for block in same]
        source = scatter(blocks, (0, 0, shape[0], shape[0]) * 2, shape)
    else:
        even = lax.ppermute(even_face, "gy", pair_swaps(count_y, 0))
        odd = lax.ppermute(odd_face, "gy", pair_swaps(count_y, 1))
        around = halos(adj_cur)
        parts = bucketed(residuals, target, recv_cell, count_x * count_y)
        source = scatter([parts] * parts.shape[0], tuple(range(parts.shape[0])), shape)
    xs = len(around) - 2
    field = jax.ShapeDtypeStruct(shape, F32)
    face = jax.ShapeDtypeStruct(shape[:2] + (LANES,), F32)
    advanced, even_face, odd_face = pl.pallas_call(
        functools.partial(first_kernel, sizes, xs),
        out_shape=(field, face, face),
        in_specs=[VMEM] * (6 + len(around)),
        out_specs=(VMEM, VMEM, VMEM),
        name="first_step",
    )(adj_cur, adj_prev, velocity, source, *around, even, odd)
    even = lax.ppermute(even_face, "gy", pair_swaps(count_y, 0))
    odd = lax.ppermute(odd_face, "gy", pair_swaps(count_y, 1))
    around = halos(advanced)
    latest, gradient = pl.pallas_call(
        functools.partial(second_kernel, sizes, xs),
        out_shape=(field, field),
        in_specs=[VMEM] * (7 + len(around)),
        out_specs=(VMEM, VMEM),
        name="second_step",
    )(advanced, adj_cur, velocity, source, fwd_accel, *around, even, odd)
    return advanced, latest, gradient


def solution(mesh):
    placed = (
        P("gx", "gz", "gy"),
        P("gx", "gz", "gy"),
        P("gx", "gz", "gy"),
        P(None, "gx", "gz", "gy"),
        P(None, ("gx", "gy", "gz")),
        P(("gx", "gy", "gz"), None),
        P(("gx", "gy", "gz")),
    )
    return jax.shard_map(
        shards,
        mesh=mesh,
        in_specs=placed,
        out_specs=(P("gx", "gz", "gy"), P("gx", "gz", "gy"), P("gx", "gz", "gy")),
        check_vma=False,
    )
```

```python
import functools
import jax
import jax.numpy as jnp
from jax import lax
from jax.experimental import pallas as pl
from jax.experimental.pallas import tpu as pltpu
from jax.sharding import PartitionSpec as P

stencil_weights = (-205.0 / 72.0, 8.0 / 5.0, -1.0 / 5.0, 8.0 / 315.0, -1.0 / 560.0)
courant_scale = 0.1
LANES = 128
F32 = jnp.float32
BF16 = jnp.bfloat16
VMEM = pl.BlockSpec(memory_space=pltpu.VMEM)
HBM = pl.BlockSpec(memory_space=pltpu.HBM)


def near(values):
    return [pltpu.with_memory_space_constraint(value, pltpu.VMEM) for value in values]


def pair_swaps(size, offset):
    pairs = []
    for i in range(offset, size - 1, 2):
        pairs += [(i, i + 1), (i + 1, i)]
    return pairs


def full_swaps(count_x, size, offset):
    pairs = pair_swaps(size, offset)
    partner = dict(pairs)
    places = [(x, i) for x in range(count_x) for i in range(size)]
    return [
        (x * size + i, x * size + partner[i] if i in partner else (x ^ 1) * size + i) for x, i in places
    ]


def xor_swaps(size, bits):
    return [(i, i ^ bits) for i in range(size)]


def pack_kernel(cur_ref, res_ref, tile_ref, cell_ref, even_ref, odd_ref, own_ref, copy_ref, res, tile, cell, sem):
    is_odd = lax.rem(lax.axis_index("gy"), 2)
    last = cur_ref.shape[2] - LANES
    start_even = pl.multiple_of((1 - is_odd) * last, LANES)
    start_odd = pl.multiple_of(is_odd * last, LANES)
    size_x = cur_ref.shape[0]
    pairs = (
        (res_ref, res),
        (tile_ref, tile),
        (cell_ref, cell),
        (cur_ref.at[:, :, pl.ds(start_even, LANES)], even_ref.at[0:size_x]),
        (cur_ref.at[:, :, pl.ds(start_odd, LANES)], odd_ref.at[0:size_x]),
        (cur_ref, copy_ref),
    )
    copies = [pltpu.make_async_copy(*pair, sem.at[i]) for i, pair in enumerate(pairs)]
    for copy in copies:
        copy.start()
    for copy in copies[:3]:
        copy.wait()
    rows = (
        res[0:1, 0:LANES], res[0:1, LANES:], res[1:2, 0:LANES], res[1:2, LANES:],
        tile[...].astype(F32), cell[...].astype(F32),
    )
    payload = jnp.concatenate(rows, axis=0)
    even_ref[size_x] = payload
    odd_ref[size_x] = payload
    own_ref[0] = payload
    for copy in copies[3:]:
        copy.wait()


def pack(cur, residuals, tile, cell):
    size_x, size_z, _ = cur.shape
    message = pltpu.VMEM((size_x + 1, size_z, LANES), F32)
    return pl.pallas_call(
        pack_kernel,
        out_shape=(message, message, pltpu.VMEM((1, 8, LANES), F32), pltpu.VMEM(cur.shape, F32)),
        in_specs=[pl.BlockSpec(memory_space=pl.ANY)] * 4,
        out_specs=(VMEM,) * 4,
        scratch_shapes=[
            pltpu.VMEM(residuals.shape, F32),
            pltpu.VMEM(tile.shape, jnp.int32),
            pltpu.VMEM(cell.shape, jnp.int32),
            pltpu.SemaphoreType.DMA((6,)),
        ],
        name="pack",
    )(cur, residuals, tile, cell)


def scattered(blocks, shape, left_ref, right_ref):
    size_x, size_z, size_y = shape
    rows = size_x * size_z
    mine = (lax.axis_index("gx") * lax.axis_size("gy") + lax.axis_index("gy")).astype(F32)
    row_iota = lax.broadcasted_iota(jnp.int32, (rows, LANES), 0)
    column_iota = lax.broadcasted_iota(jnp.int32, (size_y, LANES), 0)
    place = 0
    for block in blocks:
        cell = block[6:8].astype(jnp.int32)
        column = lax.rem(cell, size_y)
        row = jnp.where(block[4:6] == mine, lax.div(cell, size_y), -1)
        high = block[0:4].astype(BF16).astype(F32)
        rest = block[0:4] - high
        middle = rest.astype(BF16).astype(F32)
        low = rest - middle
        for half in range(2):
            lanes = slice(place, place + LANES)
            hit = row_iota == row[half : half + 1]
            for moment in range(2):
                line = 2 * moment + half
                for piece, value in enumerate((high, middle, low)):
                    top = (3 * moment + piece) * rows
                    left_ref[top : top + rows, lanes] = jnp.where(hit, value[line : line + 1], 0.0).astype(BF16)
            right_ref[:, lanes] = jnp.where(column_iota == column[half : half + 1], 1.0, 0.0).astype(BF16)
            place += LANES
    total = lax.dot_general(
        left_ref[...], right_ref[...], (((1,), (1,)), ((), ())), preferred_element_type=F32
    )
    parts = [total[i * rows : (i + 1) * rows].reshape(shape) for i in range(6)]
    return [parts[3 * moment] + (parts[3 * moment + 1] + parts[3 * moment + 2]) for moment in range(2)]


def one_hot_scratch(shape, blocks):
    count = 2 * LANES * blocks
    return [pltpu.VMEM((6 * shape[0] * shape[1], count), BF16), pltpu.VMEM((shape[2], count), BF16)]


def scatter_kernel(picks, based, *refs):
    blocks, refs = refs[: len(picks)], refs[len(picks) :]
    base_ref, refs = (refs[0], refs[1:]) if based else (None, refs)
    out_ref, left_ref, right_ref = refs
    values = [ref[pick] for ref, pick in zip(blocks, picks)]
    for moment, field in enumerate(scattered(values, out_ref.shape[1:], left_ref, right_ref)):
        out_ref[moment] = base_ref[moment] + field if based else field


def scatter(blocks, picks, shape, base=()):
    operands = near([*blocks, *base])
    return pl.pallas_call(
        functools.partial(scatter_kernel, picks, len(base)),
        out_shape=pltpu.VMEM((2,) + shape, F32),
        in_specs=[VMEM] * len(operands),
        out_specs=VMEM,
        scratch_shapes=one_hot_scratch(shape, len(picks)),
        name="scatter",
    )(*operands)


def faces_kernel(cur_ref, even_ref, odd_ref):
    half = cur_ref.shape[0] // 2
    is_odd = lax.rem(lax.axis_index("gz"), 2) == 1
    for where in column_blocks(cur_ref.shape[2]):
        low, high = cur_ref[0:half, :, where], cur_ref[half:, :, where]
        upper = lax.broadcasted_iota(jnp.int32, low.shape, 1) < 4
        first = jnp.where(upper, low, pltpu.roll(high, 4, 1))
        last = jnp.where(upper, pltpu.roll(low, 4, 1), high)
        even_ref[:, :, where] = jnp.where(is_odd, first, last)
        odd_ref[:, :, where] = jnp.where(is_odd, last, first)


def faces_z(cur):
    face = pltpu.VMEM((cur.shape[0] // 2,) + cur.shape[1:], F32)
    return call(faces_kernel, "faces_z", [cur], [face, face], (), 40000000)


def gather_kernel(picks, *refs):
    for place, pick in enumerate(picks):
        refs[-1][place] = refs[place][pick]


def gather_blocks(blocks, picks):
    return pl.pallas_call(
        functools.partial(gather_kernel, picks),
        out_shape=pltpu.VMEM((len(blocks), 8, LANES), F32),
        in_specs=[VMEM] * len(blocks),
        out_specs=VMEM,
        name="gather_blocks",
    )(*near(blocks))


def column_blocks(size_y):
    return [slice(start, start + LANES) for start in range(0, size_y, LANES)]


def pick_side(parts, is_odd, before):
    first, second = (parts[0], parts[1]) if before else (parts[1], parts[0])
    return jnp.where(is_odd, first, second)


def along_columns(count_y, cur_ref, y_refs):
    size_x, size_z, size_y = cur_ref.shape
    place = lax.axis_index("gy")
    is_odd = lax.rem(place, 2) == 1
    lane = lax.broadcasted_iota(jnp.int32, (size_x, size_z, LANES), 2)
    ends = []
    for before in (True, False):
        face = pick_side([ref[0:size_x] for ref in y_refs], is_odd, before)
        ends.append(jnp.where(place == (0 if before else count_y - 1), 0.0, face))
    wheres = column_blocks(size_y)
    columns = [ends[0]] + [cur_ref[:, :, where] for where in wheres] + [ends[1]]
    for j, where in enumerate(wheres):
        left, centre, right = columns[j : j + 3]
        total = (3.0 * stencil_weights[0]) * centre
        for offset in range(1, 5):
            pair = pltpu.roll(jnp.where(lane >= offset, centre, right), LANES - offset, 2)
            pair += pltpu.roll(jnp.where(lane < LANES - offset, centre, left), offset, 2)
            total += stencil_weights[offset] * pair
        yield where, centre, total


def across_columns(count_z, cur_ref, x_refs, z_refs):
    size_x, size_z, size_y = cur_ref.shape
    odd_x, odd_z = [lax.rem(lax.axis_index(name), 2) == 1 for name in ("gx", "gz")]
    layer = lax.broadcasted_iota(jnp.int32, (size_x, size_z, LANES), 1)
    upper = layer[0 : size_x // 2] < 4
    place_z = lax.axis_index("gz")
    for where in column_blocks(size_y):
        centre = cur_ref[:, :, where]
        halves = []
        for before in (True, False):
            layers = slice(size_x - 4, size_x) if before else slice(0, 4)
            parts = [ref[layers, :, where] for ref in x_refs]
            if len(parts) == 1:
                parts.append(jnp.zeros_like(parts[0]))
            halves.append(pick_side(parts, odd_x, before))
        along_x = jnp.concatenate([halves[0], centre, halves[1]], axis=0)
        parts = [ref[:, :, where] for ref in z_refs]
        after = jnp.where(place_z == count_z - 1, 0.0, pick_side(parts, odd_z, False))
        before = jnp.where(place_z == 0, 0.0, pick_side(parts, odd_z, True))
        low = jnp.where(upper, after, pltpu.roll(before, 4, 1))
        high = jnp.where(upper, pltpu.roll(after, 4, 1), before)
        beyond = jnp.concatenate([low, high], axis=0)
        total = jnp.zeros_like(centre)
        for offset in range(1, 5):
            pair = along_x[4 + offset : 4 + offset + size_x] + along_x[4 - offset : 4 - offset + size_x]
            pair += pltpu.roll(jnp.where(layer >= offset, centre, beyond), size_z - offset, 1)
            pair += pltpu.roll(jnp.where(layer < size_z - offset, centre, beyond), offset, 1)
            total += stencil_weights[offset] * pair
        yield where, centre, total


def first_kernel(counts, cur_ref, prev_ref, vel_ref, src_ref, even_ref, odd_ref, *refs):
    count_x, count_z, count_y = counts
    x_refs, z_refs, (next_ref, even_out, odd_out) = refs[:count_x], refs[count_x : count_x + 2], refs[count_x + 2 :]
    along = along_columns(count_y, cur_ref, (even_ref, odd_ref))
    across = across_columns(count_z, cur_ref, x_refs, z_refs)
    for (where, centre, total), (_, _, more) in zip(along, across):
        scaled = vel_ref[:, :, where] * courant_scale
        next_ref[:, :, where] = (
            2.0 * centre - prev_ref[:, :, where] + scaled * scaled * (total + more) + src_ref[0, :, :, where]
        )
    is_odd = lax.rem(lax.axis_index("gy"), 2) == 1
    first, last = next_ref[:, :, 0:LANES], next_ref[:, :, next_ref.shape[2] - LANES :]
    even_out[...] = jnp.where(is_odd, first, last)
    odd_out[...] = jnp.where(is_odd, last, first)


def second_start_kernel(counts, cur_ref, prev_ref, vel_ref, src_ref, accel_ref, *refs):
    count_x, count_z, _ = counts
    x_refs, z_refs, refs = refs[:count_x], refs[count_x : count_x + 2], refs[count_x + 2 :]
    out_ref, part_ref, speed_ref, sum_ref, factor_ref, sem = refs
    copy = pltpu.make_async_copy(cur_ref, out_ref, sem)
    copy.start()
    for where, centre, laplacian in across_columns(count_z, cur_ref, x_refs, z_refs):
        velocity = vel_ref[:, :, where]
        scaled = velocity * courant_scale
        speed_sq = scaled * scaled
        part_ref[:, :, where] = 2.0 * centre - prev_ref[:, :, where] + speed_sq * laplacian + src_ref[1, :, :, where]
        speed_ref[:, :, where] = speed_sq
        weight = -2.0 / (velocity * velocity * velocity)
        sum_ref[:, :, where] = weight * accel_ref[0, :, :, where] * centre
        factor_ref[:, :, where] = weight * accel_ref[1, :, :, where]
    copy.wait()


def second_end_kernel(
    counts, cur_ref, part_ref, speed_ref, sum_ref, factor_ref, even_ref, odd_ref,
    next_out, gradient_out, next_ref, gradient_ref, sem,
):
    copies = []
    for place, (where, _, laplacian) in enumerate(along_columns(counts[2], cur_ref, (even_ref, odd_ref))):
        advanced = part_ref[:, :, where] + speed_ref[:, :, where] * laplacian
        next_ref[place] = advanced
        gradient_ref[place] = sum_ref[:, :, where] + factor_ref[:, :, where] * advanced
        for ref, out_ref, i in ((next_ref, next_out, 0), (gradient_ref, gradient_out, 1)):
            copies.append(pltpu.make_async_copy(ref.at[place], out_ref.at[:, :, where], sem.at[2 * place + i]))
            copies[-1].start()
    for copy in copies:
        copy.wait()


def call(kernel, name, operands, outputs, scratch=(), cost=0):
    estimate = pl.CostEstimate(flops=0, bytes_accessed=cost, transcendentals=0) if cost else None
    return pl.pallas_call(
        kernel,
        out_shape=tuple(outputs),
        in_specs=[VMEM] * len(operands),
        out_specs=tuple(HBM if isinstance(output, jax.ShapeDtypeStruct) else VMEM for output in outputs),
        scratch_shapes=list(scratch),
        cost_estimate=estimate,
        name=name,
    )(*near(operands))


def bucketed(residuals, target, cell, tile_count):
    held_count = residuals.shape[1]
    capacity = max(2, 2 * held_count // tile_count)
    one_hot = (target[:, None] == jnp.arange(tile_count, dtype=jnp.int32)[None, :]).astype(jnp.int32)
    earlier = jnp.cumsum(one_hot, axis=0) - one_hot
    slot_index = target * capacity + jnp.sum(one_hot * earlier, axis=1)
    payload = jnp.stack([residuals[0], residuals[1], cell.astype(F32)])
    outgoing = jnp.zeros((3, tile_count * capacity), F32).at[:, slot_index].set(payload)
    incoming = lax.all_to_all(outgoing, ("gx", "gy"), split_axis=1, concat_axis=1, tiled=True)
    block = 2 * LANES
    count = -(-incoming.shape[1] // block)
    incoming = jnp.pad(incoming, ((0, 0), (0, count * block - incoming.shape[1])))
    mine = (lax.axis_index("gx") * lax.axis_size("gy") + lax.axis_index("gy")).astype(F32)
    parts = jnp.concatenate([incoming[:2], jnp.full((1, count * block), mine), incoming[2:]])
    return parts.reshape(4, count, 2, LANES).transpose(1, 0, 2, 3).reshape(count, 8, LANES)


def shards(adj_prev, adj_cur, velocity, fwd_accel, residuals, recv_tile, recv_cell):
    count_x, count_z, count_y = sizes = tuple(lax.axis_size(name) for name in ("gx", "gz", "gy"))
    shape = velocity.shape
    target = recv_tile[:, 0]

    def swap_faces(face, axis, size, offset):
        if count_x % 2 or (offset == 0 and size % 2 == 0):
            return lax.ppermute(face, axis, pair_swaps(size, offset))
        return lax.ppermute(face, ("gx", axis), full_swaps(count_x, size, offset))

    def halos_x(value):
        return [lax.ppermute(value, "gx", pair_swaps(count_x, offset)) for offset in range(min(2, count_x - 1))]

    def halos_z(value):
        return [swap_faces(face, "gz", count_z, offset) for offset, face in enumerate(faces_z(value))]

    even_face, odd_face, own, current = pack(
        adj_cur, residuals, target.reshape(2, LANES), recv_cell.reshape(2, LANES)
    )
    if count_x == 2 and count_y == 4:
        even = lax.ppermute(even_face, "gy", xor_swaps(4, 1))
        odd = lax.ppermute(odd_face, "gy", xor_swaps(4, 3))
        far = lax.ppermute(own, "gy", xor_swaps(4, 2))
        along_z = halos_z(current)
        same, picks = [own, far, even, odd], (0, 0, shape[0], shape[0])
        packed = gather_blocks(same, picks)
        packed, late = lax.optimization_barrier((packed, current))
        along_x = halos_x(late)
        swapped = lax.ppermute(packed, "gx", pair_swaps(2, 0))
        source = scatter(same, picks, shape)
        source = scatter([swapped] * len(same), tuple(range(len(same))), shape, [source])
    else:
        along_x, along_z = halos_x(current), halos_z(current)
        even = lax.ppermute(even_face, "gy", pair_swaps(count_y, 0))
        odd = lax.ppermute(odd_face, "gy", pair_swaps(count_y, 1))
        parts = bucketed(residuals, target, recv_cell, count_x * count_y)
        source = scatter([parts] * parts.shape[0], tuple(range(parts.shape[0])), shape)
    counts = (len(along_x), count_z, count_y)
    field, face = pltpu.VMEM(shape, F32), pltpu.VMEM(shape[:2] + (LANES,), F32)
    whole = jax.ShapeDtypeStruct(shape, F32)
    advanced, even_face, odd_face = call(
        functools.partial(first_kernel, counts),
        "first_step",
        [current, adj_prev, velocity, source, even, odd, *along_x, *along_z],
        [field, face, face],
    )
    along_x, along_z = halos_x(advanced), halos_z(advanced)
    odd = swap_faces(odd_face, "gy", count_y, 1)
    even = swap_faces(even_face, "gy", count_y, 0)
    first, *parts = call(
        functools.partial(second_start_kernel, counts),
        "second_start",
        [advanced, current, velocity, source, fwd_accel, *along_x, *along_z],
        [whole, field, field, field, field],
        [pltpu.SemaphoreType.DMA],
    )
    blocks = shape[2] // LANES
    tiles = pltpu.VMEM((blocks,) + shape[:2] + (LANES,), F32)
    latest, gradient = call(
        functools.partial(second_end_kernel, counts),
        "second_end",
        [advanced, *parts, even, odd],
        [whole, whole],
        [tiles, tiles, pltpu.SemaphoreType.DMA((2 * blocks,))],
    )
    return first, latest, gradient


def solution(mesh):
    placed = (
        P("gx", "gz", "gy"),
        P("gx", "gz", "gy"),
        P("gx", "gz", "gy"),
        P(None, "gx", "gz", "gy"),
        P(None, ("gx", "gy", "gz")),
        P(("gx", "gy", "gz"), None),
        P(("gx", "gy", "gz")),
    )
    return jax.shard_map(
        shards,
        mesh=mesh,
        in_specs=placed,
        out_specs=(P("gx", "gz", "gy"), P("gx", "gz", "gy"), P("gx", "gz", "gy")),
        check_vma=False,
    )
```

```python
import functools
import jax
import jax.numpy as jnp
from jax import lax
from jax.experimental import pallas as pl
from jax.experimental.pallas import tpu as pltpu
from jax.sharding import PartitionSpec as P

stencil_weights = (-205.0 / 72.0, 8.0 / 5.0, -1.0 / 5.0, 8.0 / 315.0, -1.0 / 560.0)
courant_scale = 0.1
LANES = 128
F32 = jnp.float32
BF16 = jnp.bfloat16
VMEM = pl.BlockSpec(memory_space=pltpu.VMEM)
HBM = pl.BlockSpec(memory_space=pltpu.HBM)


def near(values):
    return [pltpu.with_memory_space_constraint(value, pltpu.VMEM) for value in values]


def pair_swaps(size, offset):
    pairs = []
    for i in range(offset, size - 1, 2):
        pairs += [(i, i + 1), (i + 1, i)]
    return pairs


def full_swaps(count_x, size, offset):
    pairs = pair_swaps(size, offset)
    partner = dict(pairs)
    places = [(x, i) for x in range(count_x) for i in range(size)]
    return [
        (x * size + i, x * size + partner[i] if i in partner else (x ^ 1) * size + i) for x, i in places
    ]


def xor_swaps(size, bits):
    return [(i, i ^ bits) for i in range(size)]


def pack_kernel(cur_ref, res_ref, tile_ref, cell_ref, even_ref, odd_ref, own_ref, copy_ref, res, tile, cell, sem):
    is_odd = lax.rem(lax.axis_index("gy"), 2)
    last = cur_ref.shape[2] - LANES
    start_even = pl.multiple_of((1 - is_odd) * last, LANES)
    start_odd = pl.multiple_of(is_odd * last, LANES)
    size_x = cur_ref.shape[0]
    pairs = (
        (res_ref, res),
        (tile_ref, tile),
        (cell_ref, cell),
        (cur_ref.at[:, :, pl.ds(start_even, LANES)], even_ref.at[0:size_x]),
        (cur_ref.at[:, :, pl.ds(start_odd, LANES)], odd_ref.at[0:size_x]),
        (cur_ref, copy_ref),
    )
    copies = [pltpu.make_async_copy(*pair, sem.at[i]) for i, pair in enumerate(pairs)]
    for copy in copies:
        copy.start()
    for copy in copies[:3]:
        copy.wait()
    rows = (
        res[0:1, 0:LANES], res[0:1, LANES:], res[1:2, 0:LANES], res[1:2, LANES:],
        tile[...].astype(F32), cell[...].astype(F32),
    )
    payload = jnp.concatenate(rows, axis=0)
    even_ref[size_x] = payload
    odd_ref[size_x] = payload
    own_ref[0] = payload
    for copy in copies[3:]:
        copy.wait()


def pack(cur, residuals, tile, cell):
    size_x, size_z, _ = cur.shape
    message = pltpu.VMEM((size_x + 1, size_z, LANES), F32)
    return pl.pallas_call(
        pack_kernel,
        out_shape=(message, message, pltpu.VMEM((1, 8, LANES), F32), pltpu.VMEM(cur.shape, F32)),
        in_specs=[pl.BlockSpec(memory_space=pl.ANY)] * 4,
        out_specs=(VMEM,) * 4,
        scratch_shapes=[
            pltpu.VMEM(residuals.shape, F32),
            pltpu.VMEM(tile.shape, jnp.int32),
            pltpu.VMEM(cell.shape, jnp.int32),
            pltpu.SemaphoreType.DMA((6,)),
        ],
        name="pack",
    )(cur, residuals, tile, cell)


def scattered(blocks, shape, left_ref, right_ref):
    size_x, size_z, size_y = shape
    rows = size_x * size_z
    mine = (lax.axis_index("gx") * lax.axis_size("gy") + lax.axis_index("gy")).astype(F32)
    row_iota = lax.broadcasted_iota(jnp.int32, (rows, LANES), 0)
    column_iota = lax.broadcasted_iota(jnp.int32, (size_y, LANES), 0)
    place = 0
    for block in blocks:
        cell = block[6:8].astype(jnp.int32)
        column = lax.rem(cell, size_y)
        row = jnp.where(block[4:6] == mine, lax.div(cell, size_y), -1)
        high = block[0:4].astype(BF16).astype(F32)
        rest = block[0:4] - high
        middle = rest.astype(BF16).astype(F32)
        low = rest - middle
        for half in range(2):
            lanes = slice(place, place + LANES)
            hit = row_iota == row[half : half + 1]
            for moment in range(2):
                line = 2 * moment + half
                for piece, value in enumerate((high, middle, low)):
                    top = (3 * moment + piece) * rows
                    left_ref[top : top + rows, lanes] = jnp.where(hit, value[line : line + 1], 0.0).astype(BF16)
            right_ref[:, lanes] = jnp.where(column_iota == column[half : half + 1], 1.0, 0.0).astype(BF16)
            place += LANES
    total = lax.dot_general(
        left_ref[...], right_ref[...], (((1,), (1,)), ((), ())), preferred_element_type=F32
    )
    parts = [total[i * rows : (i + 1) * rows].reshape(shape) for i in range(6)]
    return [parts[3 * moment] + (parts[3 * moment + 1] + parts[3 * moment + 2]) for moment in range(2)]


def one_hot_scratch(shape, blocks):
    count = 2 * LANES * blocks
    return [pltpu.VMEM((6 * shape[0] * shape[1], count), BF16), pltpu.VMEM((shape[2], count), BF16)]


def scatter_kernel(picks, based, *refs):
    blocks, refs = refs[: len(picks)], refs[len(picks) :]
    base_ref, refs = (refs[0], refs[1:]) if based else (None, refs)
    out_ref, left_ref, right_ref = refs
    values = [ref[pick] for ref, pick in zip(blocks, picks)]
    for moment, field in enumerate(scattered(values, out_ref.shape[1:], left_ref, right_ref)):
        out_ref[moment] = base_ref[moment] + field if based else field


def scatter(blocks, picks, shape, base=()):
    operands = near([*blocks, *base])
    return pl.pallas_call(
        functools.partial(scatter_kernel, picks, len(base)),
        out_shape=pltpu.VMEM((2,) + shape, F32),
        in_specs=[VMEM] * len(operands),
        out_specs=VMEM,
        scratch_shapes=one_hot_scratch(shape, len(picks)),
        name="scatter",
    )(*operands)


def faces_kernel(cur_ref, even_ref, odd_ref, *x_refs):
    half = cur_ref.shape[0] // 2
    is_odd = lax.rem(lax.axis_index("gz"), 2) == 1
    at_odd_x = lax.rem(lax.axis_index("gx"), 2) == 1
    for where in column_blocks(cur_ref.shape[2]):
        low, high = cur_ref[0:half, :, where], cur_ref[half:, :, where]
        upper = lax.broadcasted_iota(jnp.int32, low.shape, 1) < 4
        first = jnp.where(upper, low, pltpu.roll(high, 4, 1))
        last = jnp.where(upper, pltpu.roll(low, 4, 1), high)
        even_ref[:, :, where] = jnp.where(is_odd, first, last)
        odd_ref[:, :, where] = jnp.where(is_odd, last, first)
        first, last = cur_ref[0:4, :, where], cur_ref[cur_ref.shape[0] - 4 :, :, where]
        for ref, mine, other in zip(x_refs, (last, first), (first, last)):
            ref[:, :, where] = jnp.where(at_odd_x, other, mine)


def faces_xz(cur, count_x):
    face_z = pltpu.VMEM((cur.shape[0] // 2,) + cur.shape[1:], F32)
    face_x = pltpu.VMEM((4,) + cur.shape[1:], F32)
    return call(faces_kernel, "faces", [cur], [face_z, face_z] + [face_x] * count_x)


def gather_kernel(picks, *refs):
    for place, pick in enumerate(picks):
        refs[-1][place] = refs[place][pick]


def gather_blocks(blocks, picks):
    return pl.pallas_call(
        functools.partial(gather_kernel, picks),
        out_shape=pltpu.VMEM((len(blocks), 8, LANES), F32),
        in_specs=[VMEM] * len(blocks),
        out_specs=VMEM,
        name="gather_blocks",
    )(*near(blocks))


def column_blocks(size_y):
    return [slice(start, start + LANES) for start in range(0, size_y, LANES)]


def pick_side(parts, is_odd, before):
    first, second = (parts[0], parts[1]) if before else (parts[1], parts[0])
    return jnp.where(is_odd, first, second)


def along_columns(count_y, cur_ref, y_refs):
    size_x, size_z, size_y = cur_ref.shape
    place = lax.axis_index("gy")
    is_odd = lax.rem(place, 2) == 1
    lane = lax.broadcasted_iota(jnp.int32, (size_x, size_z, LANES), 2)
    ends = []
    for before in (True, False):
        face = pick_side([ref[0:size_x] for ref in y_refs], is_odd, before)
        ends.append(jnp.where(place == (0 if before else count_y - 1), 0.0, face))
    wheres = column_blocks(size_y)
    columns = [ends[0]] + [cur_ref[:, :, where] for where in wheres] + [ends[1]]
    for j, where in enumerate(wheres):
        left, centre, right = columns[j : j + 3]
        total = (3.0 * stencil_weights[0]) * centre
        for offset in range(1, 5):
            pair = pltpu.roll(jnp.where(lane >= offset, centre, right), LANES - offset, 2)
            pair += pltpu.roll(jnp.where(lane < LANES - offset, centre, left), offset, 2)
            total += stencil_weights[offset] * pair
        yield where, centre, total


def across_columns(count_z, cur_ref, x_refs, z_refs):
    size_x, size_z, size_y = cur_ref.shape
    odd_x, odd_z = [lax.rem(lax.axis_index(name), 2) == 1 for name in ("gx", "gz")]
    layer = lax.broadcasted_iota(jnp.int32, (size_x, size_z, LANES), 1)
    upper = layer[0 : size_x // 2] < 4
    place_z = lax.axis_index("gz")
    for where in column_blocks(size_y):
        centre = cur_ref[:, :, where]
        halves = []
        for before in (True, False):
            parts = [ref[:, :, where] for ref in x_refs]
            if len(parts) == 1:
                parts.append(jnp.zeros_like(parts[0]))
            halves.append(pick_side(parts, odd_x, before))
        along_x = jnp.concatenate([halves[0], centre, halves[1]], axis=0)
        parts = [ref[:, :, where] for ref in z_refs]
        after = jnp.where(place_z == count_z - 1, 0.0, pick_side(parts, odd_z, False))
        before = jnp.where(place_z == 0, 0.0, pick_side(parts, odd_z, True))
        low = jnp.where(upper, after, pltpu.roll(before, 4, 1))
        high = jnp.where(upper, pltpu.roll(after, 4, 1), before)
        beyond = jnp.concatenate([low, high], axis=0)
        total = jnp.zeros_like(centre)
        for offset in range(1, 5):
            pair = along_x[4 + offset : 4 + offset + size_x] + along_x[4 - offset : 4 - offset + size_x]
            pair += pltpu.roll(jnp.where(layer >= offset, centre, beyond), size_z - offset, 1)
            pair += pltpu.roll(jnp.where(layer < size_z - offset, centre, beyond), offset, 1)
            total += stencil_weights[offset] * pair
        yield where, centre, total


def first_kernel(counts, cur_ref, prev_ref, vel_ref, src_ref, even_ref, odd_ref, *refs):
    count_x, count_z, count_y = counts
    x_refs, z_refs, (next_ref, even_out, odd_out) = refs[:count_x], refs[count_x : count_x + 2], refs[count_x + 2 :]
    along = along_columns(count_y, cur_ref, (even_ref, odd_ref))
    across = across_columns(count_z, cur_ref, x_refs, z_refs)
    for (where, centre, total), (_, _, more) in zip(along, across):
        scaled = vel_ref[:, :, where] * courant_scale
        next_ref[:, :, where] = (
            2.0 * centre - prev_ref[:, :, where] + scaled * scaled * (total + more) + src_ref[0, :, :, where]
        )
    is_odd = lax.rem(lax.axis_index("gy"), 2) == 1
    first, last = next_ref[:, :, 0:LANES], next_ref[:, :, next_ref.shape[2] - LANES :]
    even_out[...] = jnp.where(is_odd, first, last)
    odd_out[...] = jnp.where(is_odd, last, first)


def second_start_kernel(counts, cur_ref, prev_ref, vel_ref, src_ref, accel_ref, *refs):
    count_x, count_z, _ = counts
    x_refs, z_refs, refs = refs[:count_x], refs[count_x : count_x + 2], refs[count_x + 2 :]
    out_ref, part_ref, speed_ref, sum_ref, factor_ref, sem = refs
    copy = pltpu.make_async_copy(cur_ref, out_ref, sem)
    copy.start()
    for where, centre, laplacian in across_columns(count_z, cur_ref, x_refs, z_refs):
        velocity = vel_ref[:, :, where]
        scaled = velocity * courant_scale
        speed_sq = scaled * scaled
        part_ref[:, :, where] = 2.0 * centre - prev_ref[:, :, where] + speed_sq * laplacian + src_ref[1, :, :, where]
        speed_ref[:, :, where] = speed_sq
        weight = -2.0 / (velocity * velocity * velocity)
        sum_ref[:, :, where] = weight * accel_ref[0, :, :, where] * centre
        factor_ref[:, :, where] = weight * accel_ref[1, :, :, where]
    copy.wait()


def second_end_kernel(
    counts, cur_ref, part_ref, speed_ref, sum_ref, factor_ref, even_ref, odd_ref,
    next_out, gradient_out, next_ref, gradient_ref, sem,
):
    copies = []
    for place, (where, _, laplacian) in enumerate(along_columns(counts[2], cur_ref, (even_ref, odd_ref))):
        advanced = part_ref[:, :, where] + speed_ref[:, :, where] * laplacian
        next_ref[place] = advanced
        gradient_ref[place] = sum_ref[:, :, where] + factor_ref[:, :, where] * advanced
        for ref, out_ref, i in ((next_ref, next_out, 0), (gradient_ref, gradient_out, 1)):
            copies.append(pltpu.make_async_copy(ref.at[place], out_ref.at[:, :, where], sem.at[2 * place + i]))
            copies[-1].start()
    for copy in copies:
        copy.wait()


def call(kernel, name, operands, outputs, scratch=(), cost=0):
    estimate = pl.CostEstimate(flops=0, bytes_accessed=cost, transcendentals=0) if cost else None
    return pl.pallas_call(
        kernel,
        out_shape=tuple(outputs),
        in_specs=[VMEM] * len(operands),
        out_specs=tuple(HBM if isinstance(output, jax.ShapeDtypeStruct) else VMEM for output in outputs),
        scratch_shapes=list(scratch),
        cost_estimate=estimate,
        name=name,
    )(*near(operands))


def bucketed(residuals, target, cell, tile_count):
    held_count = residuals.shape[1]
    capacity = max(2, 2 * held_count // tile_count)
    one_hot = (target[:, None] == jnp.arange(tile_count, dtype=jnp.int32)[None, :]).astype(jnp.int32)
    earlier = jnp.cumsum(one_hot, axis=0) - one_hot
    slot_index = target * capacity + jnp.sum(one_hot * earlier, axis=1)
    payload = jnp.stack([residuals[0], residuals[1], cell.astype(F32)])
    outgoing = jnp.zeros((3, tile_count * capacity), F32).at[:, slot_index].set(payload)
    incoming = lax.all_to_all(outgoing, ("gx", "gy"), split_axis=1, concat_axis=1, tiled=True)
    block = 2 * LANES
    count = -(-incoming.shape[1] // block)
    incoming = jnp.pad(incoming, ((0, 0), (0, count * block - incoming.shape[1])))
    mine = (lax.axis_index("gx") * lax.axis_size("gy") + lax.axis_index("gy")).astype(F32)
    parts = jnp.concatenate([incoming[:2], jnp.full((1, count * block), mine), incoming[2:]])
    return parts.reshape(4, count, 2, LANES).transpose(1, 0, 2, 3).reshape(count, 8, LANES)


def shards(adj_prev, adj_cur, velocity, fwd_accel, residuals, recv_tile, recv_cell):
    count_x, count_z, count_y = sizes = tuple(lax.axis_size(name) for name in ("gx", "gz", "gy"))
    shape = velocity.shape
    target = recv_tile[:, 0]

    def swap_faces(face, axis, size, offset):
        if count_x % 2 or (offset == 0 and size % 2 == 0):
            return lax.ppermute(face, axis, pair_swaps(size, offset))
        return lax.ppermute(face, ("gx", axis), full_swaps(count_x, size, offset))

    messages_x = min(2, count_x - 1)

    def halos_x(faces):
        return [lax.ppermute(face, "gx", pair_swaps(count_x, offset)) for offset, face in enumerate(faces)]

    def halos_z(faces):
        return [swap_faces(face, "gz", count_z, offset) for offset, face in enumerate(faces)]

    even_face, odd_face, own, current = pack(
        adj_cur, residuals, target.reshape(2, LANES), recv_cell.reshape(2, LANES)
    )
    if count_x == 2 and count_y == 4:
        even = lax.ppermute(even_face, "gy", xor_swaps(4, 1))
        odd = lax.ppermute(odd_face, "gy", xor_swaps(4, 3))
        far = lax.ppermute(own, "gy", xor_swaps(4, 2))
        *faces_z, face_x = faces_xz(current, messages_x)
        along_z = halos_z(faces_z)
        same, picks = [own, far, even, odd], (0, 0, shape[0], shape[0])
        packed = gather_blocks(same, picks)
        packed, face_x = lax.optimization_barrier((packed, face_x))
        along_x = halos_x([face_x])
        swapped = lax.ppermute(packed, "gx", pair_swaps(2, 0))
        source = scatter(same, picks, shape)
        source = scatter([swapped] * len(same), tuple(range(len(same))), shape, [source])
    else:
        faces = faces_xz(current, messages_x)
        along_x, along_z = halos_x(faces[2:]), halos_z(faces[:2])
        even = lax.ppermute(even_face, "gy", pair_swaps(count_y, 0))
        odd = lax.ppermute(odd_face, "gy", pair_swaps(count_y, 1))
        parts = bucketed(residuals, target, recv_cell, count_x * count_y)
        source = scatter([parts] * parts.shape[0], tuple(range(parts.shape[0])), shape)
    counts = (messages_x, count_z, count_y)
    field, face = pltpu.VMEM(shape, F32), pltpu.VMEM(shape[:2] + (LANES,), F32)
    whole = jax.ShapeDtypeStruct(shape, F32)
    advanced, even_face, odd_face = call(
        functools.partial(first_kernel, counts),
        "first_step",
        [current, adj_prev, velocity, source, even, odd, *along_x, *along_z],
        [field, face, face],
    )
    faces = faces_xz(advanced, messages_x)
    along_x, along_z = halos_x(faces[2:]), halos_z(faces[:2])
    odd = swap_faces(odd_face, "gy", count_y, 1)
    even = swap_faces(even_face, "gy", count_y, 0)
    first, *parts = call(
        functools.partial(second_start_kernel, counts),
        "second_start",
        [advanced, current, velocity, source, fwd_accel, *along_x, *along_z],
        [whole, field, field, field, field],
        [pltpu.SemaphoreType.DMA],
    )
    blocks = shape[2] // LANES
    tiles = pltpu.VMEM((blocks,) + shape[:2] + (LANES,), F32)
    latest, gradient = call(
        functools.partial(second_end_kernel, counts),
        "second_end",
        [advanced, *parts, even, odd],
        [whole, whole],
        [tiles, tiles, pltpu.SemaphoreType.DMA((2 * blocks,))],
    )
    return first, latest, gradient


def solution(mesh):
    placed = (
        P("gx", "gz", "gy"),
        P("gx", "gz", "gy"),
        P("gx", "gz", "gy"),
        P(None, "gx", "gz", "gy"),
        P(None, ("gx", "gy", "gz")),
        P(("gx", "gy", "gz"), None),
        P(("gx", "gy", "gz")),
    )
    return jax.shard_map(
        shards,
        mesh=mesh,
        in_specs=placed,
        out_specs=(P("gx", "gz", "gy"), P("gx", "gz", "gy"), P("gx", "gz", "gy")),
        check_vma=False,
    )
```

```python
import functools
import jax
import jax.numpy as jnp
from jax import lax
from jax.experimental import pallas as pl
from jax.experimental.pallas import tpu as pltpu
from jax.sharding import PartitionSpec as P

stencil_weights = (-205.0 / 72.0, 8.0 / 5.0, -1.0 / 5.0, 8.0 / 315.0, -1.0 / 560.0)
courant_scale = 0.1
LANES = 128
F32 = jnp.float32
BF16 = jnp.bfloat16
VMEM = pl.BlockSpec(memory_space=pltpu.VMEM)
HBM = pl.BlockSpec(memory_space=pltpu.HBM)


def near(values):
    return [pltpu.with_memory_space_constraint(value, pltpu.VMEM) for value in values]


def pair_swaps(size, offset):
    pairs = []
    for i in range(offset, size - 1, 2):
        pairs += [(i, i + 1), (i + 1, i)]
    return pairs


def full_swaps(count_x, size, offset):
    pairs = pair_swaps(size, offset)
    partner = dict(pairs)
    places = [(x, i) for x in range(count_x) for i in range(size)]
    return [
        (x * size + i, x * size + partner[i] if i in partner else (x ^ 1) * size + i) for x, i in places
    ]


def xor_swaps(size, bits):
    return [(i, i ^ bits) for i in range(size)]


def pack_kernel(cur_ref, res_ref, tile_ref, cell_ref, even_ref, odd_ref, own_ref, res, tile, cell, sem):
    is_odd = lax.rem(lax.axis_index("gy"), 2)
    last = cur_ref.shape[2] - LANES
    start_even = pl.multiple_of((1 - is_odd) * last, LANES)
    start_odd = pl.multiple_of(is_odd * last, LANES)
    size_x = cur_ref.shape[0]
    pairs = (
        (res_ref, res),
        (tile_ref, tile),
        (cell_ref, cell),
        (cur_ref.at[:, :, pl.ds(start_even, LANES)], even_ref.at[0:size_x]),
        (cur_ref.at[:, :, pl.ds(start_odd, LANES)], odd_ref.at[0:size_x]),
    )
    copies = [pltpu.make_async_copy(*pair, sem.at[i]) for i, pair in enumerate(pairs)]
    for copy in copies:
        copy.start()
    for copy in copies[:3]:
        copy.wait()
    rows = (
        res[0:1, 0:LANES], res[0:1, LANES:], res[1:2, 0:LANES], res[1:2, LANES:],
        tile[...].astype(F32), cell[...].astype(F32),
    )
    payload = jnp.concatenate(rows, axis=0)
    even_ref[size_x] = payload
    odd_ref[size_x] = payload
    own_ref[0] = payload
    for copy in copies[3:]:
        copy.wait()


def pack(cur, residuals, tile, cell):
    size_x, size_z, _ = cur.shape
    message = pltpu.VMEM((size_x + 1, size_z, LANES), F32)
    return pl.pallas_call(
        pack_kernel,
        out_shape=(message, message, pltpu.VMEM((1, 8, LANES), F32)),
        in_specs=[pl.BlockSpec(memory_space=pl.ANY)] * 4,
        out_specs=(VMEM,) * 3,
        scratch_shapes=[
            pltpu.VMEM(residuals.shape, F32),
            pltpu.VMEM(tile.shape, jnp.int32),
            pltpu.VMEM(cell.shape, jnp.int32),
            pltpu.SemaphoreType.DMA((5,)),
        ],
        name="pack",
    )(cur, residuals, tile, cell)


def scattered(blocks, shape, left_ref, right_ref):
    size_x, size_z, size_y = shape
    rows = size_x * size_z
    mine = (lax.axis_index("gx") * lax.axis_size("gy") + lax.axis_index("gy")).astype(F32)
    row_iota = lax.broadcasted_iota(jnp.int32, (rows, LANES), 0).astype(BF16)
    group = min(size_y, 256)
    column_iota = lax.broadcasted_iota(jnp.int32, (group, LANES), 0).astype(BF16)
    one, zero = jnp.ones((), BF16), jnp.zeros((), BF16)
    place = 0
    for block in blocks:
        cell = block[6:8].astype(jnp.int32)
        column = lax.rem(cell, size_y)
        row = jnp.where(block[4:6] == mine, lax.div(cell, size_y), -1)
        row = row.astype(BF16)
        high = block[0:4].astype(BF16)
        rest = block[0:4] - high.astype(F32)
        middle = rest.astype(BF16)
        low = (rest - middle.astype(F32)).astype(BF16)
        for half in range(2):
            lanes = slice(place, place + LANES)
            hit = row_iota == row[half : half + 1]
            for moment in range(2):
                line = 2 * moment + half
                for piece, value in enumerate((high, middle, low)):
                    top = (3 * moment + piece) * rows
                    left_ref[top : top + rows, lanes] = jnp.where(hit, value[line : line + 1], zero)
            for start in range(0, size_y, group):
                there = column_iota == (column[half : half + 1] - start).astype(BF16)
                right_ref[start : start + group, lanes] = jnp.where(there, one, zero)
            place += LANES
    total = lax.dot_general(
        left_ref[...], right_ref[...], (((1,), (1,)), ((), ())), preferred_element_type=F32
    )
    parts = [total[i * rows : (i + 1) * rows].reshape(shape) for i in range(6)]
    return [parts[3 * moment] + (parts[3 * moment + 1] + parts[3 * moment + 2]) for moment in range(2)]


def one_hot_scratch(shape, blocks):
    count = 2 * LANES * blocks
    return [pltpu.VMEM((6 * shape[0] * shape[1], count), BF16), pltpu.VMEM((shape[2], count), BF16)]


def scatter_kernel(picks, based, *refs):
    blocks, refs = refs[: len(picks)], refs[len(picks) :]
    base_ref, refs = (refs[0], refs[1:]) if based else (None, refs)
    out_ref, left_ref, right_ref = refs
    values = [ref[pick] for ref, pick in zip(blocks, picks)]
    for moment, field in enumerate(scattered(values, out_ref.shape[1:], left_ref, right_ref)):
        out_ref[moment] = base_ref[moment] + field if based else field


def scatter(blocks, picks, shape, base=()):
    operands = near([*blocks, *base])
    return pl.pallas_call(
        functools.partial(scatter_kernel, picks, len(base)),
        out_shape=pltpu.VMEM((2,) + shape, F32),
        in_specs=[VMEM] * len(operands),
        out_specs=VMEM,
        scratch_shapes=one_hot_scratch(shape, len(picks)),
        name="scatter",
    )(*operands)


def faces_kernel(cur_ref, even_ref, odd_ref, *x_refs):
    half = cur_ref.shape[0] // 2
    is_odd = lax.rem(lax.axis_index("gz"), 2) == 1
    at_odd_x = lax.rem(lax.axis_index("gx"), 2) == 1
    for where in column_blocks(cur_ref.shape[2]):
        low, high = cur_ref[0:half, :, where], cur_ref[half:, :, where]
        upper = lax.broadcasted_iota(jnp.int32, low.shape, 1) < 4
        first = jnp.where(upper, low, pltpu.roll(high, 4, 1))
        last = jnp.where(upper, pltpu.roll(low, 4, 1), high)
        even_ref[:, :, where] = jnp.where(is_odd, first, last)
        odd_ref[:, :, where] = jnp.where(is_odd, last, first)
        first, last = cur_ref[0:4, :, where], cur_ref[cur_ref.shape[0] - 4 :, :, where]
        for ref, mine, other in zip(x_refs, (last, first), (first, last)):
            ref[:, :, where] = jnp.where(at_odd_x, other, mine)


def faces_xz(cur, count_x):
    face_z = pltpu.VMEM((cur.shape[0] // 2,) + cur.shape[1:], F32)
    face_x = pltpu.VMEM((4,) + cur.shape[1:], F32)
    return call(faces_kernel, "faces", [cur], [face_z, face_z] + [face_x] * count_x)


def gather_kernel(picks, *refs):
    for place, pick in enumerate(picks):
        refs[-1][place] = refs[place][pick]


def gather_blocks(blocks, picks):
    return pl.pallas_call(
        functools.partial(gather_kernel, picks),
        out_shape=pltpu.VMEM((len(blocks), 8, LANES), F32),
        in_specs=[VMEM] * len(blocks),
        out_specs=VMEM,
        name="gather_blocks",
    )(*near(blocks))


def column_blocks(size_y):
    return [slice(start, start + LANES) for start in range(0, size_y, LANES)]


def pick_side(parts, is_odd, before):
    first, second = (parts[0], parts[1]) if before else (parts[1], parts[0])
    return jnp.where(is_odd, first, second)


def along_columns(count_y, cur_ref, y_refs):
    size_x, size_z, size_y = cur_ref.shape
    place = lax.axis_index("gy")
    is_odd = lax.rem(place, 2) == 1
    lane = lax.broadcasted_iota(jnp.int32, (size_x, size_z, LANES), 2)
    ends = []
    for before in (True, False):
        width = y_refs[0].shape[2]
        nearest = slice(width - LANES, width) if before else slice(0, LANES)
        face = pick_side([ref[0:size_x, :, nearest] for ref in y_refs], is_odd, before)
        ends.append(jnp.where(place == (0 if before else count_y - 1), 0.0, face))
    wheres = column_blocks(size_y)
    columns = [ends[0]] + [cur_ref[:, :, where] for where in wheres] + [ends[1]]
    for j, where in enumerate(wheres):
        left, centre, right = columns[j : j + 3]
        total = (3.0 * stencil_weights[0]) * centre
        for offset in range(1, 5):
            pair = pltpu.roll(jnp.where(lane >= offset, centre, right), LANES - offset, 2)
            pair += pltpu.roll(jnp.where(lane < LANES - offset, centre, left), offset, 2)
            total += stencil_weights[offset] * pair
        yield where, centre, total


def across_columns(count_z, cur_ref, x_refs, z_refs):
    size_x, size_z, size_y = cur_ref.shape
    odd_x, odd_z = [lax.rem(lax.axis_index(name), 2) == 1 for name in ("gx", "gz")]
    layer = lax.broadcasted_iota(jnp.int32, (size_x, size_z, LANES), 1)
    upper = layer[0 : size_x // 2] < 4
    place_z = lax.axis_index("gz")
    for where in column_blocks(size_y):
        centre = cur_ref[:, :, where]
        halves = []
        for before in (True, False):
            parts = [ref[:, :, where] for ref in x_refs]
            if len(parts) == 1:
                parts.append(jnp.zeros_like(parts[0]))
            halves.append(pick_side(parts, odd_x, before))
        along_x = jnp.concatenate([halves[0], centre, halves[1]], axis=0)
        parts = [ref[:, :, where] for ref in z_refs]
        after = jnp.where(place_z == count_z - 1, 0.0, pick_side(parts, odd_z, False))
        before = jnp.where(place_z == 0, 0.0, pick_side(parts, odd_z, True))
        low = jnp.where(upper, after, pltpu.roll(before, 4, 1))
        high = jnp.where(upper, pltpu.roll(after, 4, 1), before)
        beyond = jnp.concatenate([low, high], axis=0)
        total = jnp.zeros_like(centre)
        for offset in range(1, 5):
            pair = along_x[4 + offset : 4 + offset + size_x] + along_x[4 - offset : 4 - offset + size_x]
            pair += pltpu.roll(jnp.where(layer >= offset, centre, beyond), size_z - offset, 1)
            pair += pltpu.roll(jnp.where(layer < size_z - offset, centre, beyond), offset, 1)
            total += stencil_weights[offset] * pair
        yield where, centre, total


def first_kernel(counts, cur_ref, prev_ref, vel_ref, src_ref, even_ref, odd_ref, *refs):
    count_x, count_z, count_y = counts
    x_refs, z_refs, (next_ref, even_out, odd_out) = refs[:count_x], refs[count_x : count_x + 2], refs[count_x + 2 :]
    along = along_columns(count_y, cur_ref, (even_ref, odd_ref))
    across = across_columns(count_z, cur_ref, x_refs, z_refs)
    for (where, centre, total), (_, _, more) in zip(along, across):
        scaled = vel_ref[:, :, where] * courant_scale
        next_ref[:, :, where] = (
            2.0 * centre - prev_ref[:, :, where] + scaled * scaled * (total + more) + src_ref[0, :, :, where]
        )
    is_odd = lax.rem(lax.axis_index("gy"), 2) == 1
    width = even_out.shape[2]
    first, last = next_ref[:, :, 0:width], next_ref[:, :, next_ref.shape[2] - width :]
    even_out[...] = jnp.where(is_odd, first, last)
    odd_out[...] = jnp.where(is_odd, last, first)


def second_start_kernel(counts, cur_ref, prev_ref, vel_ref, src_ref, accel_ref, even_ref, odd_ref, *refs):
    out_ref, part_ref, speed_ref, sum_ref, factor_ref, sem = refs
    copy = pltpu.make_async_copy(cur_ref, out_ref, sem)
    copy.start()
    for where, centre, laplacian in along_columns(counts[2], cur_ref, (even_ref, odd_ref)):
        velocity = vel_ref[:, :, where]
        scaled = velocity * courant_scale
        speed_sq = scaled * scaled
        part_ref[:, :, where] = 2.0 * centre - prev_ref[:, :, where] + speed_sq * laplacian + src_ref[1, :, :, where]
        speed_ref[:, :, where] = speed_sq
        weight = -2.0 / (velocity * velocity * velocity)
        sum_ref[:, :, where] = weight * accel_ref[0, :, :, where] * centre
        factor_ref[:, :, where] = weight * accel_ref[1, :, :, where]
    copy.wait()


def second_end_kernel(
    counts, cur_ref, part_ref, speed_ref, sum_ref, factor_ref, *refs
):
    count_x, count_z, _ = counts
    x_refs, z_refs, refs = refs[:count_x], refs[count_x : count_x + 2], refs[count_x + 2 :]
    next_out, gradient_out, next_ref, gradient_ref, sem = refs
    copies = []
    for place, (where, _, laplacian) in enumerate(across_columns(count_z, cur_ref, x_refs, z_refs)):
        advanced = part_ref[:, :, where] + speed_ref[:, :, where] * laplacian
        next_ref[place] = advanced
        gradient_ref[place] = sum_ref[:, :, where] + factor_ref[:, :, where] * advanced
        for ref, out_ref, i in ((next_ref, next_out, 0), (gradient_ref, gradient_out, 1)):
            copies.append(pltpu.make_async_copy(ref.at[place], out_ref.at[:, :, where], sem.at[2 * place + i]))
            copies[-1].start()
    for copy in copies:
        copy.wait()


def call(kernel, name, operands, outputs, scratch=(), cost=0):
    estimate = pl.CostEstimate(flops=0, bytes_accessed=cost, transcendentals=0) if cost else None
    return pl.pallas_call(
        kernel,
        out_shape=tuple(outputs),
        in_specs=[VMEM] * len(operands),
        out_specs=tuple(HBM if isinstance(output, jax.ShapeDtypeStruct) else VMEM for output in outputs),
        scratch_shapes=list(scratch),
        cost_estimate=estimate,
        name=name,
    )(*near(operands))


def bucketed(residuals, target, cell, tile_count):
    held_count = residuals.shape[1]
    capacity = max(2, 2 * held_count // tile_count)
    one_hot = (target[:, None] == jnp.arange(tile_count, dtype=jnp.int32)[None, :]).astype(jnp.int32)
    earlier = jnp.cumsum(one_hot, axis=0) - one_hot
    slot_index = target * capacity + jnp.sum(one_hot * earlier, axis=1)
    payload = jnp.stack([residuals[0], residuals[1], cell.astype(F32)])
    outgoing = jnp.zeros((3, tile_count * capacity), F32).at[:, slot_index].set(payload)
    incoming = lax.all_to_all(outgoing, ("gx", "gy"), split_axis=1, concat_axis=1, tiled=True)
    block = 2 * LANES
    count = -(-incoming.shape[1] // block)
    incoming = jnp.pad(incoming, ((0, 0), (0, count * block - incoming.shape[1])))
    mine = (lax.axis_index("gx") * lax.axis_size("gy") + lax.axis_index("gy")).astype(F32)
    parts = jnp.concatenate([incoming[:2], jnp.full((1, count * block), mine), incoming[2:]])
    return parts.reshape(4, count, 2, LANES).transpose(1, 0, 2, 3).reshape(count, 8, LANES)


def shards(adj_prev, adj_cur, velocity, fwd_accel, residuals, recv_tile, recv_cell):
    count_x, count_z, count_y = sizes = tuple(lax.axis_size(name) for name in ("gx", "gz", "gy"))
    shape = velocity.shape
    target = recv_tile[:, 0]

    def swap_faces(face, axis, size, offset):
        if count_x % 2 or (offset == 0 and size % 2 == 0):
            return lax.ppermute(face, axis, pair_swaps(size, offset))
        return lax.ppermute(face, ("gx", axis), full_swaps(count_x, size, offset))

    messages_x = min(2, count_x - 1)

    def halos_x(faces):
        return [lax.ppermute(face, "gx", pair_swaps(count_x, offset)) for offset, face in enumerate(faces)]

    def halos_z(faces):
        return [swap_faces(face, "gz", count_z, offset) for offset, face in enumerate(faces)]

    current = adj_cur
    even_face, odd_face, own = pack(
        adj_cur, residuals, target.reshape(2, LANES), recv_cell.reshape(2, LANES)
    )
    if count_x == 2 and count_y == 4:
        even = lax.ppermute(even_face, "gy", xor_swaps(4, 1))
        odd = lax.ppermute(odd_face, "gy", xor_swaps(4, 3))
        far = lax.ppermute(own, "gy", xor_swaps(4, 2))
        *faces_z, face_x = faces_xz(current, messages_x)
        along_z = halos_z(faces_z)
        same, picks = [own, far, even, odd], (0, 0, shape[0], shape[0])
        packed = gather_blocks(same, picks)
        packed, face_x = lax.optimization_barrier((packed, face_x))
        along_x = halos_x([face_x])
        swapped = lax.ppermute(packed, "gx", pair_swaps(2, 0))
        source = scatter(same, picks, shape)
        source = scatter([swapped] * len(same), tuple(range(len(same))), shape, [source])
    else:
        faces = faces_xz(current, messages_x)
        along_x, along_z = halos_x(faces[2:]), halos_z(faces[:2])
        even = lax.ppermute(even_face, "gy", pair_swaps(count_y, 0))
        odd = lax.ppermute(odd_face, "gy", pair_swaps(count_y, 1))
        parts = bucketed(residuals, target, recv_cell, count_x * count_y)
        source = scatter([parts] * parts.shape[0], tuple(range(parts.shape[0])), shape)
    counts = (messages_x, count_z, count_y)
    field, face = pltpu.VMEM(shape, F32), pltpu.VMEM(shape[:2] + (2 * LANES,), F32)
    whole = jax.ShapeDtypeStruct(shape, F32)
    advanced, even_face, odd_face = call(
        functools.partial(first_kernel, counts),
        "first_step",
        [current, adj_prev, velocity, source, even, odd, *along_x, *along_z],
        [field, face, face],
    )
    faces = faces_xz(advanced, messages_x)
    along_x, along_z = halos_x(faces[2:]), halos_z(faces[:2])
    odd = swap_faces(odd_face, "gy", count_y, 1)
    even = swap_faces(even_face, "gy", count_y, 0)
    first, *parts = call(
        functools.partial(second_start_kernel, counts),
        "second_start",
        [advanced, current, velocity, source, fwd_accel, even, odd],
        [whole, field, field, field, field],
        [pltpu.SemaphoreType.DMA],
    )
    blocks = shape[2] // LANES
    tiles = pltpu.VMEM((blocks,) + shape[:2] + (LANES,), F32)
    latest, gradient = call(
        functools.partial(second_end_kernel, counts),
        "second_end",
        [advanced, *parts, *along_x, *along_z],
        [whole, whole],
        [tiles, tiles, pltpu.SemaphoreType.DMA((2 * blocks,))],
    )
    return first, latest, gradient


def solution(mesh):
    placed = (
        P("gx", "gz", "gy"),
        P("gx", "gz", "gy"),
        P("gx", "gz", "gy"),
        P(None, "gx", "gz", "gy"),
        P(None, ("gx", "gy", "gz")),
        P(("gx", "gy", "gz"), None),
        P(("gx", "gy", "gz")),
    )
    return jax.shard_map(
        shards,
        mesh=mesh,
        in_specs=placed,
        out_specs=(P("gx", "gz", "gy"), P("gx", "gz", "gy"), P("gx", "gz", "gy")),
        check_vma=False,
    )
```

```python
import functools
import jax
import jax.numpy as jnp
from jax import lax
from jax.experimental import pallas as pl
from jax.experimental.pallas import tpu as pltpu
from jax.sharding import PartitionSpec as P

stencil_weights = (-205.0 / 72.0, 8.0 / 5.0, -1.0 / 5.0, 8.0 / 315.0, -1.0 / 560.0)
courant_scale = 0.1
LANES = 128
F32 = jnp.float32
BF16 = jnp.bfloat16
VMEM = pl.BlockSpec(memory_space=pltpu.VMEM)
HBM = pl.BlockSpec(memory_space=pltpu.HBM)


def near(values):
    return [pltpu.with_memory_space_constraint(value, pltpu.VMEM) for value in values]


def pair_swaps(size, offset):
    pairs = []
    for i in range(offset, size - 1, 2):
        pairs += [(i, i + 1), (i + 1, i)]
    return pairs


def full_swaps(count_x, size, offset):
    pairs = pair_swaps(size, offset)
    partner = dict(pairs)
    places = [(x, i) for x in range(count_x) for i in range(size)]
    return [
        (x * size + i, x * size + partner[i] if i in partner else (x ^ 1) * size + i) for x, i in places
    ]


def xor_swaps(size, bits):
    return [(i, i ^ bits) for i in range(size)]


def pack_kernel(cur_ref, res_ref, tile_ref, cell_ref, even_ref, odd_ref, own_ref, res, tile, cell, sem):
    is_odd = lax.rem(lax.axis_index("gy"), 2)
    last = cur_ref.shape[2] - LANES
    start_even = pl.multiple_of((1 - is_odd) * last, LANES)
    start_odd = pl.multiple_of(is_odd * last, LANES)
    size_x = cur_ref.shape[0]
    pairs = (
        (res_ref, res),
        (tile_ref, tile),
        (cell_ref, cell),
        (cur_ref.at[:, :, pl.ds(start_even, LANES)], even_ref.at[0:size_x]),
        (cur_ref.at[:, :, pl.ds(start_odd, LANES)], odd_ref.at[0:size_x]),
    )
    copies = [pltpu.make_async_copy(*pair, sem.at[i]) for i, pair in enumerate(pairs)]
    for copy in copies:
        copy.start()
    for copy in copies[:3]:
        copy.wait()
    rows = (
        res[0:1, 0:LANES], res[0:1, LANES:], res[1:2, 0:LANES], res[1:2, LANES:],
        tile[...].astype(F32), cell[...].astype(F32),
    )
    payload = jnp.concatenate(rows, axis=0)
    even_ref[size_x] = payload
    odd_ref[size_x] = payload
    own_ref[0] = payload
    for copy in copies[3:]:
        copy.wait()


def pack(cur, residuals, tile, cell):
    size_x, size_z, _ = cur.shape
    message = pltpu.VMEM((size_x + 1, size_z, LANES), F32)
    return pl.pallas_call(
        pack_kernel,
        out_shape=(message, message, pltpu.VMEM((1, 8, LANES), F32)),
        in_specs=[pl.BlockSpec(memory_space=pl.ANY)] * 4,
        out_specs=(VMEM,) * 3,
        scratch_shapes=[
            pltpu.VMEM(residuals.shape, F32),
            pltpu.VMEM(tile.shape, jnp.int32),
            pltpu.VMEM(cell.shape, jnp.int32),
            pltpu.SemaphoreType.DMA((5,)),
        ],
        name="pack",
    )(cur, residuals, tile, cell)


def scattered(blocks, shape, left_ref, right_ref):
    size_x, size_z, size_y = shape
    rows = size_x * size_z
    mine = (lax.axis_index("gx") * lax.axis_size("gy") + lax.axis_index("gy")).astype(F32)
    row_iota = lax.broadcasted_iota(jnp.int32, (rows, LANES), 0).astype(BF16)
    group = min(size_y, 256)
    column_iota = lax.broadcasted_iota(jnp.int32, (group, LANES), 0).astype(BF16)
    one, zero = jnp.ones((), BF16), jnp.zeros((), BF16)
    place = 0
    for block in blocks:
        cell = block[6:8].astype(jnp.int32)
        column = lax.rem(cell, size_y)
        row = jnp.where(block[4:6] == mine, lax.div(cell, size_y), -1)
        row = row.astype(BF16)
        high = block[0:4].astype(BF16)
        rest = block[0:4] - high.astype(F32)
        middle = rest.astype(BF16)
        low = (rest - middle.astype(F32)).astype(BF16)
        for half in range(2):
            lanes = slice(place, place + LANES)
            hit = row_iota == row[half : half + 1]
            for moment in range(2):
                line = 2 * moment + half
                for piece, value in enumerate((high, middle, low)):
                    top = (3 * moment + piece) * rows
                    left_ref[top : top + rows, lanes] = jnp.where(hit, value[line : line + 1], zero)
            for start in range(0, size_y, group):
                there = column_iota == (column[half : half + 1] - start).astype(BF16)
                right_ref[start : start + group, lanes] = jnp.where(there, one, zero)
            place += LANES
    total = lax.dot_general(
        left_ref[...], right_ref[...], (((1,), (1,)), ((), ())), preferred_element_type=F32
    )
    parts = [total[i * rows : (i + 1) * rows].reshape(shape) for i in range(6)]
    return [parts[3 * moment] + (parts[3 * moment + 1] + parts[3 * moment + 2]) for moment in range(2)]


def one_hot_scratch(shape, blocks):
    count = 2 * LANES * blocks
    return [pltpu.VMEM((6 * shape[0] * shape[1], count), BF16), pltpu.VMEM((shape[2], count), BF16)]


def scatter_kernel(picks, based, *refs):
    blocks, refs = refs[: len(picks)], refs[len(picks) :]
    base_ref, refs = (refs[0], refs[1:]) if based else (None, refs)
    out_ref, left_ref, right_ref = refs
    values = [ref[pick] for ref, pick in zip(blocks, picks)]
    for moment, field in enumerate(scattered(values, out_ref.shape[1:], left_ref, right_ref)):
        out_ref[moment] = base_ref[moment] + field if based else field


def scatter(blocks, picks, shape, base=()):
    operands = near([*blocks, *base])
    return pl.pallas_call(
        functools.partial(scatter_kernel, picks, len(base)),
        out_shape=pltpu.VMEM((2,) + shape, F32),
        in_specs=[VMEM] * len(operands),
        out_specs=VMEM,
        scratch_shapes=one_hot_scratch(shape, len(picks)),
        name="scatter",
    )(*operands)


def faces_kernel(cur_ref, even_ref, odd_ref, *x_refs):
    half = cur_ref.shape[0] // 2
    is_odd = lax.rem(lax.axis_index("gz"), 2) == 1
    at_odd_x = lax.rem(lax.axis_index("gx"), 2) == 1
    for where in column_blocks(cur_ref.shape[2]):
        low, high = cur_ref[0:half, :, where], cur_ref[half:, :, where]
        upper = lax.broadcasted_iota(jnp.int32, low.shape, 1) < 4
        first = jnp.where(upper, low, pltpu.roll(high, 4, 1))
        last = jnp.where(upper, pltpu.roll(low, 4, 1), high)
        even_ref[:, :, where] = jnp.where(is_odd, first, last)
        odd_ref[:, :, where] = jnp.where(is_odd, last, first)
        first, last = cur_ref[0:4, :, where], cur_ref[cur_ref.shape[0] - 4 :, :, where]
        for ref, mine, other in zip(x_refs, (last, first), (first, last)):
            ref[:, :, where] = jnp.where(at_odd_x, other, mine)


def faces_xz(cur, count_x):
    face_z = pltpu.VMEM((cur.shape[0] // 2,) + cur.shape[1:], F32)
    face_x = pltpu.VMEM((4,) + cur.shape[1:], F32)
    return call(faces_kernel, "faces", [cur], [face_z, face_z] + [face_x] * count_x)


def gather_kernel(picks, *refs):
    for place, pick in enumerate(picks):
        refs[-1][place] = refs[place][pick]


def gather_blocks(blocks, picks):
    return pl.pallas_call(
        functools.partial(gather_kernel, picks),
        out_shape=pltpu.VMEM((len(blocks), 8, LANES), F32),
        in_specs=[VMEM] * len(blocks),
        out_specs=VMEM,
        name="gather_blocks",
    )(*near(blocks))


def column_blocks(size_y):
    return [slice(start, start + LANES) for start in range(0, size_y, LANES)]


def pick_side(parts, is_odd, before):
    first, second = (parts[0], parts[1]) if before else (parts[1], parts[0])
    return jnp.where(is_odd, first, second)


def along_columns(count_y, cur_ref, y_refs):
    size_x, size_z, size_y = cur_ref.shape
    place = lax.axis_index("gy")
    is_odd = lax.rem(place, 2) == 1
    lane = lax.broadcasted_iota(jnp.int32, (size_x, size_z, LANES), 2)
    ends = []
    for before in (True, False):
        width = y_refs[0].shape[2]
        nearest = slice(width - LANES, width) if before else slice(0, LANES)
        face = pick_side([ref[0:size_x, :, nearest] for ref in y_refs], is_odd, before)
        ends.append(jnp.where(place == (0 if before else count_y - 1), 0.0, face))
    wheres = column_blocks(size_y)
    columns = [ends[0]] + [cur_ref[:, :, where] for where in wheres] + [ends[1]]
    for j, where in enumerate(wheres):
        left, centre, right = columns[j : j + 3]
        total = (3.0 * stencil_weights[0]) * centre
        for offset in range(1, 5):
            pair = pltpu.roll(jnp.where(lane >= offset, centre, right), LANES - offset, 2)
            pair += pltpu.roll(jnp.where(lane < LANES - offset, centre, left), offset, 2)
            total += stencil_weights[offset] * pair
        yield where, centre, total


def across_columns(count_z, cur_ref, x_refs, z_refs):
    size_x, size_z, size_y = cur_ref.shape
    odd_x, odd_z = [lax.rem(lax.axis_index(name), 2) == 1 for name in ("gx", "gz")]
    layer = lax.broadcasted_iota(jnp.int32, (size_x, size_z, LANES), 1)
    upper = layer[0 : size_x // 2] < 4
    place_z = lax.axis_index("gz")
    for where in column_blocks(size_y):
        centre = cur_ref[:, :, where]
        halves = []
        for before in (True, False):
            parts = [ref[:, :, where] for ref in x_refs]
            if len(parts) == 1:
                parts.append(jnp.zeros_like(parts[0]))
            halves.append(pick_side(parts, odd_x, before))
        along_x = jnp.concatenate([halves[0], centre, halves[1]], axis=0)
        parts = [ref[:, :, where] for ref in z_refs]
        after = jnp.where(place_z == count_z - 1, 0.0, pick_side(parts, odd_z, False))
        before = jnp.where(place_z == 0, 0.0, pick_side(parts, odd_z, True))
        low = jnp.where(upper, after, pltpu.roll(before, 4, 1))
        high = jnp.where(upper, pltpu.roll(after, 4, 1), before)
        beyond = jnp.concatenate([low, high], axis=0)
        total = jnp.zeros_like(centre)
        for offset in range(1, 5):
            pair = along_x[4 + offset : 4 + offset + size_x] + along_x[4 - offset : 4 - offset + size_x]
            pair += pltpu.roll(jnp.where(layer >= offset, centre, beyond), size_z - offset, 1)
            pair += pltpu.roll(jnp.where(layer < size_z - offset, centre, beyond), offset, 1)
            total += stencil_weights[offset] * pair
        yield where, centre, total


def first_start_kernel(counts, cur_ref, prev_ref, vel_ref, even_ref, odd_ref, part_ref):
    for where, centre, laplacian in along_columns(counts[2], cur_ref, (even_ref, odd_ref)):
        scaled = vel_ref[:, :, where] * courant_scale
        part_ref[:, :, where] = 2.0 * centre - prev_ref[:, :, where] + scaled * scaled * laplacian


def first_end_kernel(counts, cur_ref, vel_ref, src_ref, part_ref, *refs):
    count_x, count_z, _ = counts
    x_refs, z_refs, (next_ref, even_out, odd_out) = refs[:count_x], refs[count_x : count_x + 2], refs[count_x + 2 :]
    for where, _, laplacian in across_columns(count_z, cur_ref, x_refs, z_refs):
        scaled = vel_ref[:, :, where] * courant_scale
        next_ref[:, :, where] = part_ref[:, :, where] + scaled * scaled * laplacian + src_ref[0, :, :, where]
    is_odd = lax.rem(lax.axis_index("gy"), 2) == 1
    width = even_out.shape[2]
    first, last = next_ref[:, :, 0:width], next_ref[:, :, next_ref.shape[2] - width :]
    even_out[...] = jnp.where(is_odd, first, last)
    odd_out[...] = jnp.where(is_odd, last, first)


def second_start_kernel(counts, cur_ref, prev_ref, vel_ref, src_ref, accel_ref, even_ref, odd_ref, *refs):
    out_ref, part_ref, speed_ref, sum_ref, factor_ref, sem = refs
    copy = pltpu.make_async_copy(cur_ref, out_ref, sem)
    copy.start()
    for where, centre, laplacian in along_columns(counts[2], cur_ref, (even_ref, odd_ref)):
        velocity = vel_ref[:, :, where]
        scaled = velocity * courant_scale
        speed_sq = scaled * scaled
        part_ref[:, :, where] = 2.0 * centre - prev_ref[:, :, where] + speed_sq * laplacian + src_ref[1, :, :, where]
        speed_ref[:, :, where] = speed_sq
        weight = -2.0 / (velocity * velocity * velocity)
        sum_ref[:, :, where] = weight * accel_ref[0, :, :, where] * centre
        factor_ref[:, :, where] = weight * accel_ref[1, :, :, where]
    copy.wait()


def second_end_kernel(
    counts, cur_ref, part_ref, speed_ref, sum_ref, factor_ref, *refs
):
    count_x, count_z, _ = counts
    x_refs, z_refs, refs = refs[:count_x], refs[count_x : count_x + 2], refs[count_x + 2 :]
    next_out, gradient_out, next_ref, gradient_ref, sem = refs
    copies = []
    for place, (where, _, laplacian) in enumerate(across_columns(count_z, cur_ref, x_refs, z_refs)):
        advanced = part_ref[:, :, where] + speed_ref[:, :, where] * laplacian
        next_ref[place] = advanced
        gradient_ref[place] = sum_ref[:, :, where] + factor_ref[:, :, where] * advanced
        for ref, out_ref, i in ((next_ref, next_out, 0), (gradient_ref, gradient_out, 1)):
            copies.append(pltpu.make_async_copy(ref.at[place], out_ref.at[:, :, where], sem.at[2 * place + i]))
            copies[-1].start()
    for copy in copies:
        copy.wait()


def call(kernel, name, operands, outputs, scratch=(), cost=0):
    estimate = pl.CostEstimate(flops=0, bytes_accessed=cost, transcendentals=0) if cost else None
    return pl.pallas_call(
        kernel,
        out_shape=tuple(outputs),
        in_specs=[VMEM] * len(operands),
        out_specs=tuple(HBM if isinstance(output, jax.ShapeDtypeStruct) else VMEM for output in outputs),
        scratch_shapes=list(scratch),
        cost_estimate=estimate,
        name=name,
    )(*near(operands))


def bucketed(residuals, target, cell, tile_count):
    held_count = residuals.shape[1]
    capacity = max(2, 2 * held_count // tile_count)
    one_hot = (target[:, None] == jnp.arange(tile_count, dtype=jnp.int32)[None, :]).astype(jnp.int32)
    earlier = jnp.cumsum(one_hot, axis=0) - one_hot
    slot_index = target * capacity + jnp.sum(one_hot * earlier, axis=1)
    payload = jnp.stack([residuals[0], residuals[1], cell.astype(F32)])
    outgoing = jnp.zeros((3, tile_count * capacity), F32).at[:, slot_index].set(payload)
    incoming = lax.all_to_all(outgoing, ("gx", "gy"), split_axis=1, concat_axis=1, tiled=True)
    block = 2 * LANES
    count = -(-incoming.shape[1] // block)
    incoming = jnp.pad(incoming, ((0, 0), (0, count * block - incoming.shape[1])))
    mine = (lax.axis_index("gx") * lax.axis_size("gy") + lax.axis_index("gy")).astype(F32)
    parts = jnp.concatenate([incoming[:2], jnp.full((1, count * block), mine), incoming[2:]])
    return parts.reshape(4, count, 2, LANES).transpose(1, 0, 2, 3).reshape(count, 8, LANES)


def shards(adj_prev, adj_cur, velocity, fwd_accel, residuals, recv_tile, recv_cell):
    count_x, count_z, count_y = sizes = tuple(lax.axis_size(name) for name in ("gx", "gz", "gy"))
    shape = velocity.shape
    target = recv_tile[:, 0]

    def swap_faces(face, axis, size, offset):
        if count_x % 2 or (offset == 0 and size % 2 == 0):
            return lax.ppermute(face, axis, pair_swaps(size, offset))
        return lax.ppermute(face, ("gx", axis), full_swaps(count_x, size, offset))

    messages_x = min(2, count_x - 1)

    def halos_x(faces):
        return [lax.ppermute(face, "gx", pair_swaps(count_x, offset)) for offset, face in enumerate(faces)]

    def halos_z(faces):
        return [swap_faces(face, "gz", count_z, offset) for offset, face in enumerate(faces)]

    current = adj_cur
    even_face, odd_face, own = pack(
        adj_cur, residuals, target.reshape(2, LANES), recv_cell.reshape(2, LANES)
    )
    if count_x == 2 and count_y == 4:
        even = lax.ppermute(even_face, "gy", xor_swaps(4, 1))
        odd = lax.ppermute(odd_face, "gy", xor_swaps(4, 3))
        far = lax.ppermute(own, "gy", xor_swaps(4, 2))
        *faces_z, face_x = faces_xz(current, messages_x)
        along_z = halos_z(faces_z)
        same, picks = [own, far, even, odd], (0, 0, shape[0], shape[0])
        packed = gather_blocks(same, picks)
        packed, face_x = lax.optimization_barrier((packed, face_x))
        along_x = halos_x([face_x])
        swapped = lax.ppermute(packed, "gx", pair_swaps(2, 0))
        source = scatter(same, picks, shape)
        source = scatter([swapped] * len(same), tuple(range(len(same))), shape, [source])
    else:
        faces = faces_xz(current, messages_x)
        along_x, along_z = halos_x(faces[2:]), halos_z(faces[:2])
        even = lax.ppermute(even_face, "gy", pair_swaps(count_y, 0))
        odd = lax.ppermute(odd_face, "gy", pair_swaps(count_y, 1))
        parts = bucketed(residuals, target, recv_cell, count_x * count_y)
        source = scatter([parts] * parts.shape[0], tuple(range(parts.shape[0])), shape)
    counts = (messages_x, count_z, count_y)
    field, face = pltpu.VMEM(shape, F32), pltpu.VMEM(shape[:2] + (2 * LANES,), F32)
    whole = jax.ShapeDtypeStruct(shape, F32)
    (part,) = call(
        functools.partial(first_start_kernel, counts),
        "first_start",
        [current, adj_prev, velocity, even, odd],
        [field],
    )
    advanced, even_face, odd_face = call(
        functools.partial(first_end_kernel, counts),
        "first_end",
        [current, velocity, source, part, *along_x, *along_z],
        [field, face, face],
    )
    faces = faces_xz(advanced, messages_x)
    along_x, along_z = halos_x(faces[2:]), halos_z(faces[:2])
    odd = swap_faces(odd_face, "gy", count_y, 1)
    even = swap_faces(even_face, "gy", count_y, 0)
    first, *parts = call(
        functools.partial(second_start_kernel, counts),
        "second_start",
        [advanced, current, velocity, source, fwd_accel, even, odd],
        [whole, field, field, field, field],
        [pltpu.SemaphoreType.DMA],
    )
    blocks = shape[2] // LANES
    tiles = pltpu.VMEM((blocks,) + shape[:2] + (LANES,), F32)
    latest, gradient = call(
        functools.partial(second_end_kernel, counts),
        "second_end",
        [advanced, *parts, *along_x, *along_z],
        [whole, whole],
        [tiles, tiles, pltpu.SemaphoreType.DMA((2 * blocks,))],
    )
    return first, latest, gradient


def solution(mesh):
    placed = (
        P("gx", "gz", "gy"),
        P("gx", "gz", "gy"),
        P("gx", "gz", "gy"),
        P(None, "gx", "gz", "gy"),
        P(None, ("gx", "gy", "gz")),
        P(("gx", "gy", "gz"), None),
        P(("gx", "gy", "gz")),
    )
    return jax.shard_map(
        shards,
        mesh=mesh,
        in_specs=placed,
        out_specs=(P("gx", "gz", "gy"), P("gx", "gz", "gy"), P("gx", "gz", "gy")),
        check_vma=False,
    )
```

```python
import functools
import jax
import jax.numpy as jnp
from jax import lax
from jax.experimental import pallas as pl
from jax.experimental.pallas import tpu as pltpu
from jax.sharding import PartitionSpec as P

stencil_weights = (-205.0 / 72.0, 8.0 / 5.0, -1.0 / 5.0, 8.0 / 315.0, -1.0 / 560.0)
courant_scale = 0.1
LANES = 128
F32 = jnp.float32
BF16 = jnp.bfloat16
VMEM = pl.BlockSpec(memory_space=pltpu.VMEM)
HBM = pl.BlockSpec(memory_space=pltpu.HBM)


def near(values):
    return [pltpu.with_memory_space_constraint(value, pltpu.VMEM) for value in values]


def pair_swaps(size, offset):
    pairs = []
    for i in range(offset, size - 1, 2):
        pairs += [(i, i + 1), (i + 1, i)]
    return pairs


def full_swaps(count_x, size, offset):
    pairs = pair_swaps(size, offset)
    partner = dict(pairs)
    places = [(x, i) for x in range(count_x) for i in range(size)]
    return [
        (x * size + i, x * size + partner[i] if i in partner else (x ^ 1) * size + i) for x, i in places
    ]


def xor_swaps(size, bits):
    return [(i, i ^ bits) for i in range(size)]


def pack_kernel(cur_ref, res_ref, tile_ref, cell_ref, even_ref, odd_ref, own_ref, res, tile, cell, sem):
    is_odd = lax.rem(lax.axis_index("gy"), 2)
    last = cur_ref.shape[2] - LANES
    start_even = pl.multiple_of((1 - is_odd) * last, LANES)
    start_odd = pl.multiple_of(is_odd * last, LANES)
    size_x = cur_ref.shape[0]
    pairs = (
        (res_ref, res),
        (tile_ref, tile),
        (cell_ref, cell),
        (cur_ref.at[:, :, pl.ds(start_even, LANES)], even_ref.at[0:size_x]),
        (cur_ref.at[:, :, pl.ds(start_odd, LANES)], odd_ref.at[0:size_x]),
    )
    copies = [pltpu.make_async_copy(*pair, sem.at[i]) for i, pair in enumerate(pairs)]
    for copy in copies:
        copy.start()
    for copy in copies[:3]:
        copy.wait()
    rows = (
        res[0:1, 0:LANES], res[0:1, LANES:], res[1:2, 0:LANES], res[1:2, LANES:],
        tile[...].astype(F32), cell[...].astype(F32),
    )
    payload = jnp.concatenate(rows, axis=0)
    even_ref[size_x] = payload
    odd_ref[size_x] = payload
    own_ref[0] = payload
    for copy in copies[3:]:
        copy.wait()


def pack(cur, residuals, tile, cell):
    size_x, size_z, _ = cur.shape
    message = pltpu.VMEM((size_x + 1, size_z, LANES), F32)
    return pl.pallas_call(
        pack_kernel,
        out_shape=(message, message, pltpu.VMEM((1, 8, LANES), F32)),
        in_specs=[pl.BlockSpec(memory_space=pl.ANY)] * 4,
        out_specs=(VMEM,) * 3,
        scratch_shapes=[
            pltpu.VMEM(residuals.shape, F32),
            pltpu.VMEM(tile.shape, jnp.int32),
            pltpu.VMEM(cell.shape, jnp.int32),
            pltpu.SemaphoreType.DMA((5,)),
        ],
        name="pack",
    )(cur, residuals, tile, cell)


def scattered(blocks, shape, left_ref, right_ref):
    size_x, size_z, size_y = shape
    rows = size_x * size_z
    mine = (lax.axis_index("gx") * lax.axis_size("gy") + lax.axis_index("gy")).astype(F32)
    row_iota = lax.broadcasted_iota(jnp.int32, (rows, LANES), 0).astype(BF16)
    group = min(size_y, 256)
    column_iota = lax.broadcasted_iota(jnp.int32, (group, LANES), 0).astype(BF16)
    one, zero = jnp.ones((), BF16), jnp.zeros((), BF16)
    place = 0
    for block in blocks:
        cell = block[6:8].astype(jnp.int32)
        column = lax.rem(cell, size_y)
        row = jnp.where(block[4:6] == mine, lax.div(cell, size_y), -1)
        row = row.astype(BF16)
        high = block[0:4].astype(BF16)
        rest = block[0:4] - high.astype(F32)
        middle = rest.astype(BF16)
        low = (rest - middle.astype(F32)).astype(BF16)
        for half in range(2):
            lanes = slice(place, place + LANES)
            hit = row_iota == row[half : half + 1]
            for moment in range(2):
                line = 2 * moment + half
                for piece, value in enumerate((high, middle, low)):
                    top = (3 * moment + piece) * rows
                    left_ref[top : top + rows, lanes] = jnp.where(hit, value[line : line + 1], zero)
            for start in range(0, size_y, group):
                there = column_iota == (column[half : half + 1] - start).astype(BF16)
                right_ref[start : start + group, lanes] = jnp.where(there, one, zero)
            place += LANES
    total = lax.dot_general(
        left_ref[...], right_ref[...], (((1,), (1,)), ((), ())), preferred_element_type=F32
    )
    parts = [total[i * rows : (i + 1) * rows].reshape(shape) for i in range(6)]
    return [parts[3 * moment] + (parts[3 * moment + 1] + parts[3 * moment + 2]) for moment in range(2)]


def one_hot_scratch(shape, blocks):
    count = 2 * LANES * blocks
    return [pltpu.VMEM((6 * shape[0] * shape[1], count), BF16), pltpu.VMEM((shape[2], count), BF16)]


def scatter_kernel(picks, based, *refs):
    blocks, refs = refs[: len(picks)], refs[len(picks) :]
    base_ref, refs = (refs[0], refs[1:]) if based else (None, refs)
    out_ref, left_ref, right_ref = refs
    values = [ref[pick] for ref, pick in zip(blocks, picks)]
    for moment, field in enumerate(scattered(values, out_ref.shape[1:], left_ref, right_ref)):
        out_ref[moment] = base_ref[moment] + field if based else field


def scatter(blocks, picks, shape, base=()):
    operands = near([*blocks, *base])
    return pl.pallas_call(
        functools.partial(scatter_kernel, picks, len(base)),
        out_shape=pltpu.VMEM((2,) + shape, F32),
        in_specs=[VMEM] * len(operands),
        out_specs=VMEM,
        scratch_shapes=one_hot_scratch(shape, len(picks)),
        name="scatter",
    )(*operands)


def faces_kernel(cur_ref, even_ref, odd_ref, *x_refs):
    half = cur_ref.shape[0] // 2
    is_odd = lax.rem(lax.axis_index("gz"), 2) == 1
    at_odd_x = lax.rem(lax.axis_index("gx"), 2) == 1
    for where in column_blocks(cur_ref.shape[2]):
        low, high = cur_ref[0:half, :, where], cur_ref[half:, :, where]
        upper = lax.broadcasted_iota(jnp.int32, low.shape, 1) < 4
        first = jnp.where(upper, low, pltpu.roll(high, 4, 1))
        last = jnp.where(upper, pltpu.roll(low, 4, 1), high)
        even_ref[:, :, where] = jnp.where(is_odd, first, last)
        odd_ref[:, :, where] = jnp.where(is_odd, last, first)
        first, last = cur_ref[0:4, :, where], cur_ref[cur_ref.shape[0] - 4 :, :, where]
        for ref, mine, other in zip(x_refs, (last, first), (first, last)):
            ref[:, :, where] = jnp.where(at_odd_x, other, mine)


def faces_xz(cur, count_x):
    face_z = pltpu.VMEM((cur.shape[0] // 2,) + cur.shape[1:], F32)
    face_x = pltpu.VMEM((4,) + cur.shape[1:], F32)
    return call(faces_kernel, "faces", [cur], [face_z, face_z] + [face_x] * count_x)


def gather_kernel(picks, *refs):
    for place, pick in enumerate(picks):
        refs[-1][place] = refs[place][pick]


def gather_blocks(blocks, picks):
    return pl.pallas_call(
        functools.partial(gather_kernel, picks),
        out_shape=pltpu.VMEM((len(blocks), 8, LANES), F32),
        in_specs=[VMEM] * len(blocks),
        out_specs=VMEM,
        name="gather_blocks",
    )(*near(blocks))


def column_blocks(size_y):
    return [slice(start, start + LANES) for start in range(0, size_y, LANES)]


def pick_side(parts, is_odd, before):
    first, second = (parts[0], parts[1]) if before else (parts[1], parts[0])
    return jnp.where(is_odd, first, second)


def along_columns(count_y, cur_ref, y_refs):
    size_x, size_z, size_y = cur_ref.shape
    place = lax.axis_index("gy")
    is_odd = lax.rem(place, 2) == 1
    lane = lax.broadcasted_iota(jnp.int32, (size_x, size_z, LANES), 2)
    ends = []
    for before in (True, False):
        width = y_refs[0].shape[2]
        nearest = slice(width - LANES, width) if before else slice(0, LANES)
        face = pick_side([ref[0:size_x, :, nearest] for ref in y_refs], is_odd, before)
        ends.append(jnp.where(place == (0 if before else count_y - 1), 0.0, face))
    wheres = column_blocks(size_y)
    columns = [ends[0]] + [cur_ref[:, :, where] for where in wheres] + [ends[1]]
    for j, where in enumerate(wheres):
        left, centre, right = columns[j : j + 3]
        total = (3.0 * stencil_weights[0]) * centre
        for offset in range(1, 5):
            pair = pltpu.roll(jnp.where(lane >= offset, centre, right), LANES - offset, 2)
            pair += pltpu.roll(jnp.where(lane < LANES - offset, centre, left), offset, 2)
            total += stencil_weights[offset] * pair
        yield where, centre, total


def across_columns(count_z, cur_ref, x_refs, z_refs):
    size_x, size_z, size_y = cur_ref.shape
    odd_x, odd_z = [lax.rem(lax.axis_index(name), 2) == 1 for name in ("gx", "gz")]
    layer = lax.broadcasted_iota(jnp.int32, (size_x, size_z, LANES), 1)
    upper = layer[0 : size_x // 2] < 4
    place_z = lax.axis_index("gz")
    for where in column_blocks(size_y):
        centre = cur_ref[:, :, where]
        halves = []
        for before in (True, False):
            parts = [ref[:, :, where] for ref in x_refs]
            if len(parts) == 1:
                parts.append(jnp.zeros_like(parts[0]))
            halves.append(pick_side(parts, odd_x, before))
        along_x = jnp.concatenate([halves[0], centre, halves[1]], axis=0)
        parts = [ref[:, :, where] for ref in z_refs]
        after = jnp.where(place_z == count_z - 1, 0.0, pick_side(parts, odd_z, False))
        before = jnp.where(place_z == 0, 0.0, pick_side(parts, odd_z, True))
        low = jnp.where(upper, after, pltpu.roll(before, 4, 1))
        high = jnp.where(upper, pltpu.roll(after, 4, 1), before)
        beyond = jnp.concatenate([low, high], axis=0)
        total = jnp.zeros_like(centre)
        for offset in range(1, 5):
            pair = along_x[4 + offset : 4 + offset + size_x] + along_x[4 - offset : 4 - offset + size_x]
            pair += pltpu.roll(jnp.where(layer >= offset, centre, beyond), size_z - offset, 1)
            pair += pltpu.roll(jnp.where(layer < size_z - offset, centre, beyond), offset, 1)
            total += stencil_weights[offset] * pair
        yield where, centre, total


def first_start_kernel(counts, cur_ref, prev_ref, vel_ref, even_ref, odd_ref, part_ref):
    for where, centre, laplacian in along_columns(counts[2], cur_ref, (even_ref, odd_ref)):
        scaled = vel_ref[:, :, where] * courant_scale
        part_ref[:, :, where] = 2.0 * centre - prev_ref[:, :, where] + scaled * scaled * laplacian


def first_end_kernel(counts, cur_ref, vel_ref, src_ref, part_ref, *refs):
    count_x, count_z, _ = counts
    x_refs, z_refs, (next_ref, even_out, odd_out) = refs[:count_x], refs[count_x : count_x + 2], refs[count_x + 2 :]
    for where, _, laplacian in across_columns(count_z, cur_ref, x_refs, z_refs):
        scaled = vel_ref[:, :, where] * courant_scale
        next_ref[:, :, where] = part_ref[:, :, where] + scaled * scaled * laplacian + src_ref[0, :, :, where]
    is_odd = lax.rem(lax.axis_index("gy"), 2) == 1
    width = even_out.shape[2]
    first, last = next_ref[:, :, 0:width], next_ref[:, :, next_ref.shape[2] - width :]
    even_out[...] = jnp.where(is_odd, first, last)
    odd_out[...] = jnp.where(is_odd, last, first)


def second_start_kernel(counts, cur_ref, prev_ref, vel_ref, src_ref, accel_ref, even_ref, odd_ref, *refs):
    part_ref, speed_ref, sum_ref, factor_ref = refs
    for where, centre, laplacian in along_columns(counts[2], cur_ref, (even_ref, odd_ref)):
        velocity = vel_ref[:, :, where]
        scaled = velocity * courant_scale
        speed_sq = scaled * scaled
        part_ref[:, :, where] = 2.0 * centre - prev_ref[:, :, where] + speed_sq * laplacian + src_ref[1, :, :, where]
        speed_ref[:, :, where] = speed_sq
        weight = -2.0 / (velocity * velocity * velocity)
        sum_ref[:, :, where] = weight * accel_ref[0, :, :, where] * centre
        factor_ref[:, :, where] = weight * accel_ref[1, :, :, where]


def second_end_kernel(
    counts, cur_ref, part_ref, speed_ref, sum_ref, factor_ref, *refs
):
    count_x, count_z, _ = counts
    x_refs, z_refs, refs = refs[:count_x], refs[count_x : count_x + 2], refs[count_x + 2 :]
    out_ref, next_out, gradient_out, next_ref, gradient_ref, sem = refs
    copies = [pltpu.make_async_copy(cur_ref, out_ref, sem.at[sem.shape[0] - 1])]
    copies[0].start()
    for place, (where, _, laplacian) in enumerate(across_columns(count_z, cur_ref, x_refs, z_refs)):
        advanced = part_ref[:, :, where] + speed_ref[:, :, where] * laplacian
        next_ref[place] = advanced
        gradient_ref[place] = sum_ref[:, :, where] + factor_ref[:, :, where] * advanced
        for ref, out_ref, i in ((next_ref, next_out, 0), (gradient_ref, gradient_out, 1)):
            copies.append(pltpu.make_async_copy(ref.at[place], out_ref.at[:, :, where], sem.at[2 * place + i]))
            copies[-1].start()
    for copy in copies:
        copy.wait()


def call(kernel, name, operands, outputs, scratch=(), cost=0):
    estimate = pl.CostEstimate(flops=0, bytes_accessed=cost, transcendentals=0) if cost else None
    return pl.pallas_call(
        kernel,
        out_shape=tuple(outputs),
        in_specs=[VMEM] * len(operands),
        out_specs=tuple(HBM if isinstance(output, jax.ShapeDtypeStruct) else VMEM for output in outputs),
        scratch_shapes=list(scratch),
        cost_estimate=estimate,
        name=name,
    )(*near(operands))


def bucketed(residuals, target, cell, tile_count):
    held_count = residuals.shape[1]
    capacity = max(2, 2 * held_count // tile_count)
    one_hot = (target[:, None] == jnp.arange(tile_count, dtype=jnp.int32)[None, :]).astype(jnp.int32)
    earlier = jnp.cumsum(one_hot, axis=0) - one_hot
    slot_index = target * capacity + jnp.sum(one_hot * earlier, axis=1)
    payload = jnp.stack([residuals[0], residuals[1], cell.astype(F32)])
    outgoing = jnp.zeros((3, tile_count * capacity), F32).at[:, slot_index].set(payload)
    incoming = lax.all_to_all(outgoing, ("gx", "gy"), split_axis=1, concat_axis=1, tiled=True)
    block = 2 * LANES
    count = -(-incoming.shape[1] // block)
    incoming = jnp.pad(incoming, ((0, 0), (0, count * block - incoming.shape[1])))
    mine = (lax.axis_index("gx") * lax.axis_size("gy") + lax.axis_index("gy")).astype(F32)
    parts = jnp.concatenate([incoming[:2], jnp.full((1, count * block), mine), incoming[2:]])
    return parts.reshape(4, count, 2, LANES).transpose(1, 0, 2, 3).reshape(count, 8, LANES)


def shards(adj_prev, adj_cur, velocity, fwd_accel, residuals, recv_tile, recv_cell):
    count_x, count_z, count_y = sizes = tuple(lax.axis_size(name) for name in ("gx", "gz", "gy"))
    shape = velocity.shape
    target = recv_tile[:, 0]

    def swap_faces(face, axis, size, offset):
        if count_x % 2 or (offset == 0 and size % 2 == 0):
            return lax.ppermute(face, axis, pair_swaps(size, offset))
        return lax.ppermute(face, ("gx", axis), full_swaps(count_x, size, offset))

    messages_x = min(2, count_x - 1)

    def halos_x(faces):
        return [lax.ppermute(face, "gx", pair_swaps(count_x, offset)) for offset, face in enumerate(faces)]

    def halos_z(faces):
        return [swap_faces(face, "gz", count_z, offset) for offset, face in enumerate(faces)]

    current = adj_cur
    even_face, odd_face, own = pack(
        adj_cur, residuals, target.reshape(2, LANES), recv_cell.reshape(2, LANES)
    )
    if count_x == 2 and count_y == 4:
        even = lax.ppermute(even_face, "gy", xor_swaps(4, 1))
        odd = lax.ppermute(odd_face, "gy", xor_swaps(4, 3))
        far = lax.ppermute(own, "gy", xor_swaps(4, 2))
        *faces_z, face_x = faces_xz(current, messages_x)
        along_z = halos_z(faces_z)
        same, picks = [own, far, even, odd], (0, 0, shape[0], shape[0])
        packed = gather_blocks(same, picks)
        packed, face_x = lax.optimization_barrier((packed, face_x))
        along_x = halos_x([face_x])
        swapped = lax.ppermute(packed, "gx", pair_swaps(2, 0))
        source = scatter(same, picks, shape)
        source = scatter([swapped] * len(same), tuple(range(len(same))), shape, [source])
    else:
        faces = faces_xz(current, messages_x)
        along_x, along_z = halos_x(faces[2:]), halos_z(faces[:2])
        even = lax.ppermute(even_face, "gy", pair_swaps(count_y, 0))
        odd = lax.ppermute(odd_face, "gy", pair_swaps(count_y, 1))
        parts = bucketed(residuals, target, recv_cell, count_x * count_y)
        source = scatter([parts] * parts.shape[0], tuple(range(parts.shape[0])), shape)
    counts = (messages_x, count_z, count_y)
    field, face = pltpu.VMEM(shape, F32), pltpu.VMEM(shape[:2] + (2 * LANES,), F32)
    whole = jax.ShapeDtypeStruct(shape, F32)
    (part,) = call(
        functools.partial(first_start_kernel, counts),
        "first_start",
        [current, adj_prev, velocity, even, odd],
        [field],
    )
    advanced, even_face, odd_face = call(
        functools.partial(first_end_kernel, counts),
        "first_end",
        [current, velocity, source, part, *along_x, *along_z],
        [field, face, face],
    )
    faces = faces_xz(advanced, messages_x)
    along_x, along_z = halos_x(faces[2:]), halos_z(faces[:2])
    odd = swap_faces(odd_face, "gy", count_y, 1)
    even = swap_faces(even_face, "gy", count_y, 0)
    parts = call(
        functools.partial(second_start_kernel, counts),
        "second_start",
        [advanced, current, velocity, source, fwd_accel, even, odd],
        [field, field, field, field],
    )
    blocks = shape[2] // LANES
    tiles = pltpu.VMEM((blocks,) + shape[:2] + (LANES,), F32)
    first, latest, gradient = call(
        functools.partial(second_end_kernel, counts),
        "second_end",
        [advanced, *parts, *along_x, *along_z],
        [whole, whole, whole],
        [tiles, tiles, pltpu.SemaphoreType.DMA((2 * blocks + 1,))],
    )
    return first, latest, gradient


def solution(mesh):
    placed = (
        P("gx", "gz", "gy"),
        P("gx", "gz", "gy"),
        P("gx", "gz", "gy"),
        P(None, "gx", "gz", "gy"),
        P(None, ("gx", "gy", "gz")),
        P(("gx", "gy", "gz"), None),
        P(("gx", "gy", "gz")),
    )
    return jax.shard_map(
        shards,
        mesh=mesh,
        in_specs=placed,
        out_specs=(P("gx", "gz", "gy"), P("gx", "gz", "gy"), P("gx", "gz", "gy")),
        check_vma=False,
    )
```

```python
import functools
import jax
import jax.numpy as jnp
from jax import lax
from jax.experimental import pallas as pl
from jax.experimental.pallas import tpu as pltpu
from jax.sharding import PartitionSpec as P

stencil_weights = (-205.0 / 72.0, 8.0 / 5.0, -1.0 / 5.0, 8.0 / 315.0, -1.0 / 560.0)
courant_scale = 0.1
LANES = 128
F32 = jnp.float32
BF16 = jnp.bfloat16
VMEM = pl.BlockSpec(memory_space=pltpu.VMEM)
HBM = pl.BlockSpec(memory_space=pltpu.HBM)


def near(values):
    return [pltpu.with_memory_space_constraint(value, pltpu.VMEM) for value in values]


def pair_swaps(size, offset):
    pairs = []
    for i in range(offset, size - 1, 2):
        pairs += [(i, i + 1), (i + 1, i)]
    return pairs


def full_swaps(count_x, size, offset):
    pairs = pair_swaps(size, offset)
    partner = dict(pairs)
    places = [(x, i) for x in range(count_x) for i in range(size)]
    return [
        (x * size + i, x * size + partner[i] if i in partner else (x ^ 1) * size + i) for x, i in places
    ]


def xor_swaps(size, bits):
    return [(i, i ^ bits) for i in range(size)]


def pack_kernel(cur_ref, res_ref, tile_ref, cell_ref, even_ref, odd_ref, own_ref, res, tile, cell, sem):
    is_odd = lax.rem(lax.axis_index("gy"), 2)
    last = cur_ref.shape[2] - LANES
    start_even = pl.multiple_of((1 - is_odd) * last, LANES)
    start_odd = pl.multiple_of(is_odd * last, LANES)
    size_x = cur_ref.shape[0]
    pairs = (
        (res_ref, res),
        (tile_ref, tile),
        (cell_ref, cell),
        (cur_ref.at[:, :, pl.ds(start_even, LANES)], even_ref.at[0:size_x]),
        (cur_ref.at[:, :, pl.ds(start_odd, LANES)], odd_ref.at[0:size_x]),
    )
    copies = [pltpu.make_async_copy(*pair, sem.at[i]) for i, pair in enumerate(pairs)]
    for copy in copies:
        copy.start()
    for copy in copies[:3]:
        copy.wait()
    rows = (
        res[0:1, 0:LANES], res[0:1, LANES:], res[1:2, 0:LANES], res[1:2, LANES:],
        tile[...].astype(F32), cell[...].astype(F32),
    )
    payload = jnp.concatenate(rows, axis=0)
    even_ref[size_x] = payload
    odd_ref[size_x] = payload
    own_ref[0] = payload
    for copy in copies[3:]:
        copy.wait()


def pack(cur, residuals, tile, cell):
    size_x, size_z, _ = cur.shape
    message = pltpu.VMEM((size_x + 1, size_z, LANES), F32)
    return pl.pallas_call(
        pack_kernel,
        out_shape=(message, message, pltpu.VMEM((1, 8, LANES), F32)),
        in_specs=[pl.BlockSpec(memory_space=pl.ANY)] * 4,
        out_specs=(VMEM,) * 3,
        scratch_shapes=[
            pltpu.VMEM(residuals.shape, F32),
            pltpu.VMEM(tile.shape, jnp.int32),
            pltpu.VMEM(cell.shape, jnp.int32),
            pltpu.SemaphoreType.DMA((5,)),
        ],
        name="pack",
    )(cur, residuals, tile, cell)


def scattered(blocks, shape, left_ref, right_ref):
    size_x, size_z, size_y = shape
    rows = size_x * size_z
    mine = (lax.axis_index("gx") * lax.axis_size("gy") + lax.axis_index("gy")).astype(F32)
    row_iota = lax.broadcasted_iota(jnp.int32, (rows, LANES), 0).astype(BF16)
    group = min(size_y, 256)
    column_iota = lax.broadcasted_iota(jnp.int32, (group, LANES), 0).astype(BF16)
    one, zero = jnp.ones((), BF16), jnp.zeros((), BF16)
    place = 0
    for block in blocks:
        cell = block[6:8].astype(jnp.int32)
        column = lax.rem(cell, size_y)
        row = jnp.where(block[4:6] == mine, lax.div(cell, size_y), -1)
        row = row.astype(BF16)
        high = block[0:4].astype(BF16)
        rest = block[0:4] - high.astype(F32)
        middle = rest.astype(BF16)
        low = (rest - middle.astype(F32)).astype(BF16)
        for half in range(2):
            lanes = slice(place, place + LANES)
            hit = row_iota == row[half : half + 1]
            for moment in range(2):
                line = 2 * moment + half
                for piece, value in enumerate((high, middle, low)):
                    top = (3 * moment + piece) * rows
                    left_ref[top : top + rows, lanes] = jnp.where(hit, value[line : line + 1], zero)
            for start in range(0, size_y, group):
                there = column_iota == (column[half : half + 1] - start).astype(BF16)
                right_ref[start : start + group, lanes] = jnp.where(there, one, zero)
            place += LANES
    total = lax.dot_general(
        left_ref[...], right_ref[...], (((1,), (1,)), ((), ())), preferred_element_type=F32
    )
    parts = [total[i * rows : (i + 1) * rows].reshape(shape) for i in range(6)]
    return [parts[3 * moment] + (parts[3 * moment + 1] + parts[3 * moment + 2]) for moment in range(2)]


def one_hot_scratch(shape, blocks):
    count = 2 * LANES * blocks
    return [pltpu.VMEM((6 * shape[0] * shape[1], count), BF16), pltpu.VMEM((shape[2], count), BF16)]


def scatter_kernel(picks, based, *refs):
    blocks, refs = refs[: len(picks)], refs[len(picks) :]
    base_ref, refs = (refs[0], refs[1:]) if based else (None, refs)
    out_ref, left_ref, right_ref = refs
    values = [ref[pick] for ref, pick in zip(blocks, picks)]
    for moment, field in enumerate(scattered(values, out_ref.shape[1:], left_ref, right_ref)):
        out_ref[moment] = base_ref[moment] + field if based else field


def scatter(blocks, picks, shape, base=()):
    operands = near([*blocks, *base])
    return pl.pallas_call(
        functools.partial(scatter_kernel, picks, len(base)),
        out_shape=pltpu.VMEM((2,) + shape, F32),
        in_specs=[VMEM] * len(operands),
        out_specs=VMEM,
        scratch_shapes=one_hot_scratch(shape, len(picks)),
        name="scatter",
    )(*operands)


def faces_kernel(cur_ref, even_ref, odd_ref, *x_refs):
    half = cur_ref.shape[0] // 2
    is_odd = lax.rem(lax.axis_index("gz"), 2) == 1
    at_odd_x = lax.rem(lax.axis_index("gx"), 2) == 1
    for where in column_blocks(cur_ref.shape[2]):
        low, high = cur_ref[0:half, :, where], cur_ref[half:, :, where]
        upper = lax.broadcasted_iota(jnp.int32, low.shape, 1) < 4
        first = jnp.where(upper, low, pltpu.roll(high, 4, 1))
        last = jnp.where(upper, pltpu.roll(low, 4, 1), high)
        even_ref[:, :, where] = jnp.where(is_odd, first, last)
        odd_ref[:, :, where] = jnp.where(is_odd, last, first)
        first, last = cur_ref[0:4, :, where], cur_ref[cur_ref.shape[0] - 4 :, :, where]
        for ref, mine, other in zip(x_refs, (last, first), (first, last)):
            ref[:, :, where] = jnp.where(at_odd_x, other, mine)


def faces_xz(cur, count_x):
    face_z = pltpu.VMEM((cur.shape[0] // 2,) + cur.shape[1:], F32)
    face_x = pltpu.VMEM((4,) + cur.shape[1:], F32)
    return call(faces_kernel, "faces", [cur], [face_z, face_z] + [face_x] * count_x)


def gather_kernel(picks, *refs):
    for place, pick in enumerate(picks):
        refs[-1][place] = refs[place][pick]


def gather_blocks(blocks, picks):
    return pl.pallas_call(
        functools.partial(gather_kernel, picks),
        out_shape=pltpu.VMEM((len(blocks), 8, LANES), F32),
        in_specs=[VMEM] * len(blocks),
        out_specs=VMEM,
        name="gather_blocks",
    )(*near(blocks))


def column_blocks(size_y):
    return [slice(start, start + LANES) for start in range(0, size_y, LANES)]


def pick_side(parts, is_odd, before):
    first, second = (parts[0], parts[1]) if before else (parts[1], parts[0])
    return jnp.where(is_odd, first, second)


def along_columns(count_y, cur_ref, y_refs):
    size_x, size_z, size_y = cur_ref.shape
    place = lax.axis_index("gy")
    is_odd = lax.rem(place, 2) == 1
    lane = lax.broadcasted_iota(jnp.int32, (size_x, size_z, LANES), 2)
    ends = []
    for before in (True, False):
        width = y_refs[0].shape[2]
        nearest = slice(width - LANES, width) if before else slice(0, LANES)
        face = pick_side([ref[0:size_x, :, nearest] for ref in y_refs], is_odd, before)
        ends.append(jnp.where(place == (0 if before else count_y - 1), 0.0, face))
    wheres = column_blocks(size_y)
    columns = [ends[0]] + [cur_ref[:, :, where] for where in wheres] + [ends[1]]
    for j, where in enumerate(wheres):
        left, centre, right = columns[j : j + 3]
        total = (3.0 * stencil_weights[0]) * centre
        for offset in range(1, 5):
            pair = pltpu.roll(jnp.where(lane >= offset, centre, right), LANES - offset, 2)
            pair += pltpu.roll(jnp.where(lane < LANES - offset, centre, left), offset, 2)
            total += stencil_weights[offset] * pair
        yield where, centre, total


def across_columns(count_z, cur_ref, x_refs, z_refs):
    size_x, size_z, size_y = cur_ref.shape
    odd_x, odd_z = [lax.rem(lax.axis_index(name), 2) == 1 for name in ("gx", "gz")]
    layer = lax.broadcasted_iota(jnp.int32, (size_x, size_z, LANES), 1)
    upper = layer[0 : size_x // 2] < 4
    place_z = lax.axis_index("gz")
    for where in column_blocks(size_y):
        centre = cur_ref[:, :, where]
        halves = []
        for before in (True, False):
            parts = [ref[:, :, where] for ref in x_refs]
            if len(parts) == 1:
                parts.append(jnp.zeros_like(parts[0]))
            halves.append(pick_side(parts, odd_x, before))
        along_x = jnp.concatenate([halves[0], centre, halves[1]], axis=0)
        parts = [ref[:, :, where] for ref in z_refs]
        after = jnp.where(place_z == count_z - 1, 0.0, pick_side(parts, odd_z, False))
        before = jnp.where(place_z == 0, 0.0, pick_side(parts, odd_z, True))
        low = jnp.where(upper, after, pltpu.roll(before, 4, 1))
        high = jnp.where(upper, pltpu.roll(after, 4, 1), before)
        beyond = jnp.concatenate([low, high], axis=0)
        total = jnp.zeros_like(centre)
        for offset in range(1, 5):
            pair = along_x[4 + offset : 4 + offset + size_x] + along_x[4 - offset : 4 - offset + size_x]
            pair += pltpu.roll(jnp.where(layer >= offset, centre, beyond), size_z - offset, 1)
            pair += pltpu.roll(jnp.where(layer < size_z - offset, centre, beyond), offset, 1)
            total += stencil_weights[offset] * pair
        yield where, centre, total


def first_start_kernel(counts, cur_ref, prev_ref, vel_ref, even_ref, odd_ref, part_ref):
    for where, centre, laplacian in along_columns(counts[2], cur_ref, (even_ref, odd_ref)):
        scaled = vel_ref[:, :, where] * courant_scale
        part_ref[:, :, where] = 2.0 * centre - prev_ref[:, :, where] + scaled * scaled * laplacian


def first_end_kernel(counts, cur_ref, vel_ref, src_ref, part_ref, *refs):
    count_x, count_z, _ = counts
    x_refs, z_refs, (next_ref, even_out, odd_out) = refs[:count_x], refs[count_x : count_x + 2], refs[count_x + 2 :]
    for where, _, laplacian in across_columns(count_z, cur_ref, x_refs, z_refs):
        scaled = vel_ref[:, :, where] * courant_scale
        next_ref[:, :, where] = part_ref[:, :, where] + scaled * scaled * laplacian + src_ref[0, :, :, where]
    is_odd = lax.rem(lax.axis_index("gy"), 2) == 1
    width = even_out.shape[2]
    first, last = next_ref[:, :, 0:width], next_ref[:, :, next_ref.shape[2] - width :]
    even_out[...] = jnp.where(is_odd, first, last)
    odd_out[...] = jnp.where(is_odd, last, first)


def second_start_kernel(counts, cur_ref, prev_ref, vel_ref, src_ref, accel_ref, even_ref, odd_ref, *refs):
    part_ref, speed_ref, sum_ref, factor_ref = refs
    for where, centre, laplacian in along_columns(counts[2], cur_ref, (even_ref, odd_ref)):
        velocity = vel_ref[:, :, where]
        scaled = velocity * courant_scale
        speed_sq = scaled * scaled
        part_ref[:, :, where] = 2.0 * centre - prev_ref[:, :, where] + speed_sq * laplacian + src_ref[1, :, :, where]
        speed_ref[:, :, where] = speed_sq
        weight = -2.0 / (velocity * velocity * velocity)
        sum_ref[:, :, where] = weight * accel_ref[0, :, :, where] * centre
        factor_ref[:, :, where] = weight * accel_ref[1, :, :, where]


def second_end_kernel(
    counts, cur_ref, part_ref, speed_ref, sum_ref, factor_ref, *refs
):
    count_x, count_z, _ = counts
    x_refs, z_refs, refs = refs[:count_x], refs[count_x : count_x + 2], refs[count_x + 2 :]
    out_ref, next_out, gradient_out, next_ref, gradient_ref, sem = refs
    copies = [pltpu.make_async_copy(cur_ref, out_ref, sem.at[sem.shape[0] - 1])]
    copies[0].start()
    for place, (where, _, laplacian) in enumerate(across_columns(count_z, cur_ref, x_refs, z_refs)):
        advanced = part_ref[:, :, where] + speed_ref[:, :, where] * laplacian
        next_ref[place] = advanced
        gradient_ref[place] = sum_ref[:, :, where] + factor_ref[:, :, where] * advanced
        for ref, out_ref, i in ((next_ref, next_out, 0), (gradient_ref, gradient_out, 1)):
            copies.append(pltpu.make_async_copy(ref.at[place], out_ref.at[:, :, where], sem.at[2 * place + i]))
            copies[-1].start()
    for copy in copies:
        copy.wait()


def call(kernel, name, operands, outputs, scratch=(), cost=0):
    estimate = pl.CostEstimate(flops=0, bytes_accessed=cost, transcendentals=0) if cost else None
    return pl.pallas_call(
        kernel,
        out_shape=tuple(outputs),
        in_specs=[VMEM] * len(operands),
        out_specs=tuple(HBM if isinstance(output, jax.ShapeDtypeStruct) else VMEM for output in outputs),
        scratch_shapes=list(scratch),
        cost_estimate=estimate,
        name=name,
    )(*near(operands))


def bucketed(residuals, target, cell, tile_count):
    held_count = residuals.shape[1]
    capacity = max(2, 2 * held_count // tile_count)
    one_hot = (target[:, None] == jnp.arange(tile_count, dtype=jnp.int32)[None, :]).astype(jnp.int32)
    earlier = jnp.cumsum(one_hot, axis=0) - one_hot
    slot_index = target * capacity + jnp.sum(one_hot * earlier, axis=1)
    payload = jnp.stack([residuals[0], residuals[1], cell.astype(F32)])
    outgoing = jnp.zeros((3, tile_count * capacity), F32).at[:, slot_index].set(payload)
    incoming = lax.all_to_all(outgoing, ("gx", "gy"), split_axis=1, concat_axis=1, tiled=True)
    block = 2 * LANES
    count = -(-incoming.shape[1] // block)
    incoming = jnp.pad(incoming, ((0, 0), (0, count * block - incoming.shape[1])))
    mine = (lax.axis_index("gx") * lax.axis_size("gy") + lax.axis_index("gy")).astype(F32)
    parts = jnp.concatenate([incoming[:2], jnp.full((1, count * block), mine), incoming[2:]])
    return parts.reshape(4, count, 2, LANES).transpose(1, 0, 2, 3).reshape(count, 8, LANES)


def shards(adj_prev, adj_cur, velocity, fwd_accel, residuals, recv_tile, recv_cell):
    count_x, count_z, count_y = sizes = tuple(lax.axis_size(name) for name in ("gx", "gz", "gy"))
    shape = velocity.shape
    target = recv_tile[:, 0]

    def swap_faces(face, axis, size, offset):
        if count_x % 2 or (offset == 0 and size % 2 == 0):
            return lax.ppermute(face, axis, pair_swaps(size, offset))
        return lax.ppermute(face, ("gx", axis), full_swaps(count_x, size, offset))

    messages_x = min(2, count_x - 1)

    def halos_x(faces):
        return [lax.ppermute(face, "gx", pair_swaps(count_x, offset)) for offset, face in enumerate(faces)]

    def halos_z(faces):
        return [swap_faces(face, "gz", count_z, offset) for offset, face in enumerate(faces)]

    current = adj_cur
    even_face, odd_face, own = pack(
        adj_cur, residuals, target.reshape(2, LANES), recv_cell.reshape(2, LANES)
    )
    if count_x == 2 and count_y == 4:
        even = lax.ppermute(even_face, "gy", xor_swaps(4, 1))
        odd = lax.ppermute(odd_face, "gy", xor_swaps(4, 3))
        far = lax.ppermute(own, "gy", xor_swaps(4, 2))
        current, own = lax.optimization_barrier((current, own))
        *faces_z, face_x = faces_xz(current, messages_x)
        along_z = halos_z(faces_z)
        same, picks = [own, far, even, odd], (0, 0, shape[0], shape[0])
        packed = gather_blocks(same, picks)
        packed, face_x = lax.optimization_barrier((packed, face_x))
        along_x = halos_x([face_x])
        swapped = lax.ppermute(packed, "gx", pair_swaps(2, 0))
        source = scatter(same, picks, shape)
        source = scatter([swapped] * len(same), tuple(range(len(same))), shape, [source])
    else:
        faces = faces_xz(current, messages_x)
        along_x, along_z = halos_x(faces[2:]), halos_z(faces[:2])
        even = lax.ppermute(even_face, "gy", pair_swaps(count_y, 0))
        odd = lax.ppermute(odd_face, "gy", pair_swaps(count_y, 1))
        parts = bucketed(residuals, target, recv_cell, count_x * count_y)
        source = scatter([parts] * parts.shape[0], tuple(range(parts.shape[0])), shape)
    counts = (messages_x, count_z, count_y)
    field, face = pltpu.VMEM(shape, F32), pltpu.VMEM(shape[:2] + (2 * LANES,), F32)
    whole = jax.ShapeDtypeStruct(shape, F32)
    (part,) = call(
        functools.partial(first_start_kernel, counts),
        "first_start",
        [current, adj_prev, velocity, even, odd],
        [field],
    )
    advanced, even_face, odd_face = call(
        functools.partial(first_end_kernel, counts),
        "first_end",
        [current, velocity, source, part, *along_x, *along_z],
        [field, face, face],
    )
    faces = faces_xz(advanced, messages_x)
    along_x, along_z = halos_x(faces[2:]), halos_z(faces[:2])
    odd = swap_faces(odd_face, "gy", count_y, 1)
    even = swap_faces(even_face, "gy", count_y, 0)
    parts = call(
        functools.partial(second_start_kernel, counts),
        "second_start",
        [advanced, current, velocity, source, fwd_accel, even, odd],
        [field, field, field, field],
    )
    blocks = shape[2] // LANES
    tiles = pltpu.VMEM((blocks,) + shape[:2] + (LANES,), F32)
    first, latest, gradient = call(
        functools.partial(second_end_kernel, counts),
        "second_end",
        [advanced, *parts, *along_x, *along_z],
        [whole, whole, whole],
        [tiles, tiles, pltpu.SemaphoreType.DMA((2 * blocks + 1,))],
    )
    return first, latest, gradient


def solution(mesh):
    placed = (
        P("gx", "gz", "gy"),
        P("gx", "gz", "gy"),
        P("gx", "gz", "gy"),
        P(None, "gx", "gz", "gy"),
        P(None, ("gx", "gy", "gz")),
        P(("gx", "gy", "gz"), None),
        P(("gx", "gy", "gz")),
    )
    return jax.shard_map(
        shards,
        mesh=mesh,
        in_specs=placed,
        out_specs=(P("gx", "gz", "gy"), P("gx", "gz", "gy"), P("gx", "gz", "gy")),
        check_vma=False,
    )
```
